256 devices in a mesh: tm: 16 (over z, core), sx: 4 (over x), sy: 4 (over y).
Axes of the slice: x: 4, y: 4, z: 8, core: 2. Of those that a mesh axis runs over, the one named last changes fastest.
Arguments:
- slices_state: float32 [16, 64, 16, 16, 128], P('tm', None, 'sx', 'sy'), may hold values from -6 to 6
- forcing: float32 [16, 64, 16, 16, 128], P('tm', None, 'sx', 'sy'), may hold values from -0.6 to 0.6
- initial: float32 [64, 16, 16, 128], P(None, 'sx', 'sy'), may hold values from -6 to 6
- volume: float32 [64, 64], replicated, may hold values from -0.06 to 0.06
- lift: float32 [6, 64, 16], replicated, may hold values from -0.024 to 0.024
Outputs:
- corrected: float32 [16, 64, 16, 16, 128], P('tm', None, 'sx', 'sy')
- residual: float32 [16, 64, 16, 16, 128], P('tm', None, 'sx', 'sy')
The draws below stay inside these ranges and needn't reach their ends.
All inputs are finite; a program needn't handle non-finite values.
Results may differ from the reference program's by a relative error of at most 0.00018.
Values sent between devices are 32-bit elements; how exact they have to be, the bound alone decides.
No kernel may reach another device: no remote copies, remote signals or barrier semaphores. Data moves between devices by JAX's collectives and lax.ppermute only.
A program may use at most 64 MiB of HBM per device.

```python
import jax
import jax.numpy as jnp
from jax import lax

DOFS = 64
EZ = 128
SLICES = 16
NEX = 16
NEY = 16


def level_of(rng, dims, cuts, low, high):
    def one(dim, parts):
        draws = jax.random.uniform(jax.random.fold_in(jax.random.fold_in(rng, 6), dim), (parts,), jnp.float32, low / len(cuts), high / len(cuts))
        return jnp.repeat(jnp.exp(draws), dims[dim] // parts).reshape((-1,) + (1,) * (len(dims) - dim - 1))

    factor_of = one(*cuts[0])
    for cut in cuts[1:]:
        factor_of = factor_of * one(*cut)
    return factor_of


def normal_values(key, shape, scale, limit, shards=(), kind=jnp.bfloat16):
    drawn = scale * jax.random.normal(key, shape, jnp.float32)
    if shards:
        drawn = drawn * level_of(key, shape, shards, -0.22, 0.18)
    return jnp.clip(drawn, -limit, limit).astype(kind)


def setup_inputs(seed: int = 0) -> dict:
    key_of = jax.random.split(jax.random.key(seed), 6)
    return {
        "slices_state": normal_values(key_of[0], (SLICES, DOFS, NEX, NEY, EZ), 1.0, 6.0, ((0, 16), (2, 4), (3, 4)), jnp.float32),
        "forcing": normal_values(key_of[1], (SLICES, DOFS, NEX, NEY, EZ), 0.1, 0.6, ((0, 16), (2, 4), (3, 4)), jnp.float32),
        "initial": normal_values(key_of[2], (DOFS, NEX, NEY, EZ), 1.0, 6.0, ((1, 4), (2, 4)), jnp.float32),
        "volume": normal_values(key_of[3], (DOFS, DOFS), 0.01, 0.06, (), jnp.float32),
        "lift": normal_values(key_of[4], (6, DOFS, 16), 0.004, 0.024, (), jnp.float32),
    }


def lower_side(t, axis):
    count = t.shape[axis]
    zero = jnp.zeros_like(lax.slice_in_dim(t, 0, 1, axis=axis))
    return jnp.concatenate([zero, lax.slice_in_dim(t, 0, count - 1, axis=axis)], axis)


def upper_side(t, axis):
    count = t.shape[axis]
    zero = jnp.zeros_like(lax.slice_in_dim(t, 0, 1, axis=axis))
    return jnp.concatenate([lax.slice_in_dim(t, 1, count, axis=axis), zero], axis)


def delta(field, weight, lift_flat):
    width, nx, ny, nz = field.shape
    cube = field.reshape(4, 4, 4, nx, ny, nz)
    x_plus = cube[3].reshape(16, nx, ny, nz)
    x_minus = cube[0].reshape(16, nx, ny, nz)
    y_plus = cube[:, 3].reshape(16, nx, ny, nz)
    y_minus = cube[:, 0].reshape(16, nx, ny, nz)
    z_plus = cube[:, :, 3].reshape(16, nx, ny, nz)
    z_minus = cube[:, :, 0].reshape(16, nx, ny, nz)
    stacked = jnp.concatenate([lower_side(x_plus, 1), upper_side(x_minus, 1), lower_side(y_plus, 2), upper_side(y_minus, 2), lower_side(z_plus, 3), upper_side(z_minus, 3)], 0).reshape(96, -1)
    own = jnp.dot(weight, field.reshape(width, -1), precision=lax.Precision.HIGHEST, preferred_element_type=jnp.float32)
    faces = jnp.dot(lift_flat, stacked, precision=lax.Precision.HIGHEST, preferred_element_type=jnp.float32)
    return (own + faces).reshape(field.shape)


def reference(slices_state, forcing, initial, volume, lift):
    weight = volume - 0.1 * jnp.eye(volume.shape[0], dtype=jnp.float32)
    lift_flat = jnp.transpose(lift, (1, 0, 2)).reshape(volume.shape[0], 96)
    many = jax.vmap(lambda v: delta(v, weight, lift_flat))
    starts = jnp.concatenate([initial[None], slices_state[:-1]], 0)
    relaxed = starts
    for step in range(3):
        relaxed = relaxed + many(relaxed) + forcing
    residual = (relaxed + many(relaxed) + forcing) - slices_state

    def advance(carry, resid_slice):
        nxt = carry + 4.0 * delta(carry, weight, lift_flat) + resid_slice
        return nxt, nxt

    _, error = lax.scan(advance, jnp.zeros_like(initial), residual)
    corrected = slices_state + error
    return corrected, residual
```

```python
import functools

import jax
import jax.numpy as jnp
from jax import lax
from jax.experimental import pallas as pl
from jax.experimental.pallas import tpu as pltpu
from jax.sharding import Mesh, PartitionSpec as P

F32, BF16 = jnp.float32, jnp.bfloat16
AXES = ("tg", "tj", "sx", "sy")
FLAG = pl.BlockSpec(memory_space=pltpu.SMEM)
VM = pl.BlockSpec(memory_space=pltpu.VMEM)
PARAMS = pltpu.CompilerParams(vmem_limit_bytes=40 << 20)
XB, XA, YB, YA, ZB, ZA, G1, G2, G3 = range(9)


def call(kernel, out, flops, nbytes, scratch=(), smem=True):
    def run(*args):
        specs = [VM] * len(args)
        if smem:
            specs[0] = FLAG
        return pl.pallas_call(
            kernel,
            out_shape=[jax.ShapeDtypeStruct(s, d) for s, d in out],
            in_specs=specs,
            out_specs=[VM] * len(out),
            scratch_shapes=list(scratch),
            compiler_params=PARAMS,
            cost_estimate=pl.CostEstimate(flops=flops, bytes_accessed=nbytes, transcendentals=0),
        )(*args)

    return run


def split(value):
    high = value.astype(BF16)
    return high, (value - high.astype(F32)).astype(BF16)


def weights_kernel(w_ref, o_ref):
    high, low = split(w_ref[...])
    o_ref[:, 0:160] = high
    o_ref[:, 160:320] = high
    o_ref[:, 320:480] = low


def product(w, parts):
    high, low = split(jnp.concatenate(parts, 0))
    return jnp.dot(w, jnp.concatenate([high, low, high], 0), preferred_element_type=F32)


def y_trace(ref, b, t):
    return jnp.concatenate([ref[t, 16 * a + 4 * b : 16 * a + 4 * b + 4, :] for a in range(4)], 0)


def z_trace(ref, c, t):
    return ref[t, pl.ds(c, 16, stride=4), :]


def tiles(ref, rows, which):
    return jnp.concatenate([ref[t, rows, :] for t in which], 1)


def lanes(shape):
    return lax.broadcasted_iota(jnp.int32, shape, 1)


ALL = slice(None)


def given(ref, t):
    return ref[pl.ds(t, 64, stride=16), :]


def emit_faces(ref, xp, xm, yp, ym):
    for i in range(4):
        xp[i] = ref[12 + i, 48:64, :]
        xm[i] = ref[i, 0:16, :]
        yp[i] = y_trace(ref, 3, 4 * i + 3)
        ym[i] = y_trace(ref, 0, 4 * i)


def faces_kernel(v, xp, xm, yp, ym, held):
    for t in range(16):
        held[t] = given(v, t)
    emit_faces(held, xp, xm, yp, ym)


def fine_step(flags, v, source, xb, xa, yb, ya, w, store):
    weight = w[...]
    lane = lanes((16, 128))
    for i in range(4):
        row = [4 * i + j for j in range(4)]
        own = tiles(v, ALL, row)
        if i == 0:
            below_x = tiles(xb, ALL, range(4)) * flags[XB]
        else:
            below_x = tiles(v, slice(48, 64), [t - 4 for t in row])
        if i == 3:
            above_x = tiles(xa, ALL, range(4)) * flags[XA]
        else:
            above_x = tiles(v, slice(0, 16), [t + 4 for t in row])
        below_y = jnp.concatenate([yb[i] * flags[YB]] + [y_trace(v, 3, t) for t in row[:3]], 1)
        above_y = jnp.concatenate([y_trace(v, 0, t) for t in row[1:]] + [ya[i] * flags[YA]], 1)
        below_z = [jnp.where(lane == 0, 0.0, pltpu.roll(z_trace(v, 3, t), 1, 1)) for t in row]
        above_z = [jnp.where(lane == 127, 0.0, pltpu.roll(z_trace(v, 0, t), 127, 1)) for t in row]
        mixed = product(
            weight,
            [own, below_x, above_x, below_y, above_y]
            + [jnp.concatenate(below_z, 1), jnp.concatenate(above_z, 1)],
        )
        value = (own - 0.1 * own) + mixed
        for j, t in enumerate(row):
            store(t, value[:, 128 * j : 128 * j + 128] + given(source, t))


def first_fine_kernel(flags, v, source, xb, xa, yb, ya, w, out, xp, xm, yp, ym, held):
    for t in range(16):
        held[t] = given(v, t)
    fine_kernel(flags, held, source, xb, xa, yb, ya, w, out, xp, xm, yp, ym)


def fine_kernel(flags, v, source, xb, xa, yb, ya, w, out, xp, xm, yp, ym):
    def store(t, value):
        out[t] = value

    fine_step(flags, v, source, xb, xa, yb, ya, w, store)
    emit_faces(out, xp, xm, yp, ym)


def residual_kernel(flags, v, source, xb, xa, yb, ya, w, state, out, held):
    def store(t, value):
        value = value - given(state, t)
        out[pl.ds(t, 64, stride=16), :] = value
        held[t] = value

    fine_step(flags, v, source, xb, xa, yb, ya, w, store)


def coarse_plane(weight, ref, p, below_z, above_z):
    both = (2 * p, 2 * p + 1)
    own = tiles(ref, ALL, both)
    lane = lanes((16, 256))
    y = lane % 16
    y_plus = jnp.concatenate([y_trace(ref, 3, t) for t in both], 1)
    y_minus = jnp.concatenate([y_trace(ref, 0, t) for t in both], 1)
    below_x = jnp.where(lane < 16, 0.0, pltpu.roll(tiles(ref, slice(48, 64), both), 16, 1))
    above_x = jnp.where(lane >= 240, 0.0, pltpu.roll(tiles(ref, slice(0, 16), both), 240, 1))
    below_y = jnp.where(y == 0, 0.0, pltpu.roll(y_plus, 1, 1))
    above_y = jnp.where(y == 15, 0.0, pltpu.roll(y_minus, 255, 1))
    mixed = product(weight, [own, below_x, above_x, below_y, above_y, below_z, above_z])
    return (own - 0.4 * own) + 4.0 * mixed


def plane(ref, p):
    return tiles(ref, ALL, (2 * p, 2 * p + 1))


def put(ref, p, value, rows=ALL):
    ref[2 * p, rows, :] = value[:, 0:128]
    ref[2 * p + 1, rows, :] = value[:, 128:256]


def z_plane(ref, c, p):
    return jnp.concatenate([z_trace(ref, c, 2 * p), z_trace(ref, c, 2 * p + 1)], 1)


def emit_wide(ref, up, down):
    put(up, 0, plane(ref, 1), slice(0, 64))
    put(up, 0, z_plane(ref, 3, 0), slice(64, 80))
    put(down, 0, plane(ref, 0), slice(0, 64))
    put(down, 0, z_plane(ref, 0, 1), slice(64, 80))


def pair_steps(flags, v, below, above, w, extended, first, add_first, add_second, add_halo):
    weight = w[...]
    has_below, has_above = flags[ZB], flags[ZA]
    both = (0, 1)
    put(extended, 0, tiles(below, slice(0, 64), both) * has_below)
    put(extended, 1, plane(v, 0))
    put(extended, 2, plane(v, 1))
    put(extended, 3, tiles(above, slice(0, 64), both) * has_above)
    for p in range(4):
        if p == 0:
            lower = tiles(below, slice(64, 80), both) * has_below
        else:
            lower = z_plane(extended, 3, p - 1)
        if p == 3:
            upper = tiles(above, slice(64, 80), both) * has_above
        else:
            upper = z_plane(extended, 0, p + 1)
        value = coarse_plane(weight, extended, p, lower, upper)
        if p == 0:
            if add_halo:
                value = value + tiles(below, slice(80, 144), both)
            value = value * has_below
        elif p == 3:
            if add_halo:
                value = value + tiles(above, slice(80, 144), both)
            value = value * has_above
        elif add_first is not None:
            value = value + add_first(p - 1)
        put(first, p, value)
    result = []
    for p in (1, 2):
        value = coarse_plane(weight, first, p, z_plane(first, 3, p - 1), z_plane(first, 0, p + 1))
        result.append(value if add_second is None else value + add_second(p - 1))
    return result


def local_first_kernel(r, up, down):
    emit_wide(r, up, down)
    put(up, 0, plane(r, 3), slice(80, 144))
    put(down, 0, plane(r, 2), slice(80, 144))


def local_pair_kernel(flags, r, below, above, w, out, up, down, extended, first):
    result = pair_steps(
        flags, r, below, above, w, extended, first,
        lambda p: plane(r, 2 + p), lambda p: plane(r, 4 + p), True,
    )
    for p in range(2):
        put(out, p, plane(r, p))
        put(out, 2 + p, plane(first, 1 + p))
        put(out, 4 + p, result[p])
    put(up, 0, z_plane(out, 3, 5))
    put(down, 0, z_plane(out, 0, 4))


def local_last_kernel(flags, e, r, below, above, w, out, up, down):
    weight = w[...]
    for p in range(2):
        lower = plane(below, 0) * flags[ZB] if p == 0 else z_plane(e, 3, 4)
        upper = plane(above, 0) * flags[ZA] if p == 1 else z_plane(e, 0, 5)
        put(out, p, coarse_plane(weight, e, 4 + p, lower, upper) + plane(r, 6 + p))
    emit_wide(out, up, down)


def chain_kernel(flags, v, below, above, w, out, up, down, extended, first):
    result = pair_steps(flags, v, below, above, w, extended, first, None, None, False)
    for p in range(2):
        put(out, p, result[p])
    emit_wide(out, up, down)


def chain_add_kernel(flags, v, below, above, w, add, out, up, down, extended, first):
    result = pair_steps(
        flags, v, below, above, w, extended, first, None, lambda p: plane(add, p), False
    )
    for p in range(2):
        put(out, p, result[p])
    emit_wide(out, up, down)


def pick_kernel(flags, one, two, three, out, up, down):
    out[...] = one[...] * flags[G1] + two[...] * flags[G2] + three[...] * flags[G3]
    emit_wide(out, up, down)


def last_first_kernel(flags, v, below, above, w, e, out, tail, up, down, extended, first):
    result = pair_steps(flags, v, below, above, w, extended, first, None, None, False)
    for p in range(2):
        put(out, p, plane(first, 1 + p) + plane(e, p))
        put(tail, p, result[p])
        put(out, 2 + p, result[p] + plane(e, 2 + p))
    emit_wide(tail, up, down)


def last_second_kernel(flags, v, below, above, w, e, e3, out, extended, first):
    result = pair_steps(flags, v, below, above, w, extended, first, None, None, False)
    for p in range(2):
        put(out, p, plane(first, 1 + p) + plane(e, 4 + p))
        put(out, 2 + p, result[p] + plane(e3, p))


def index_of(t, x, y):
    return (t * 4 + x) * 4 + y


def ring(dt, dx, dy):
    return [
        (index_of(t, x, y), index_of((t + dt) % 16, (x + dx) % 4, (y + dy) % 4))
        for t in range(16)
        for x in range(4)
        for y in range(4)
    ]


def slab_ring(dg, ds):
    return [(64 * g + s, 64 * ((g + dg) % 4) + (s + ds) % 64) for g in range(4) for s in range(64)]


def send(value, pairs):
    return lax.ppermute(value, AXES, pairs)


def local(slices_state, forcing, initial, volume, lift):
    tg, tj = lax.axis_index("tg"), lax.axis_index("tj")
    sx, sy = lax.axis_index("sx"), lax.axis_index("sy")
    slab = (tj * 4 + sx) * 4 + sy
    tm = tg * 4 + tj
    flags = jnp.stack(
        [sx > 0, sx < 3, sy > 0, sy < 3, slab > 0, slab < 63, tg == 1, tg == 2, tg == 3]
    ).astype(F32)
    lift_flat = jnp.transpose(lift, (1, 0, 2)).reshape(64, 96)
    w = jnp.concatenate([volume, lift_flat], 1)
    face, wide, trace = ((4, 16, 128), F32), ((2, 80, 128), F32), ((2, 16, 128), F32)
    whole, two, rows = ((16, 64, 128), F32), ((4, 64, 128), F32), ((1024, 128), F32)
    (w,) = call(weights_kernel, [((64, 480), BF16)], 0, 1 << 17, smem=False)(w)

    state = slices_state.reshape(1024, 128)
    source = forcing.reshape(1024, 128)
    leaving = jnp.where(tm == 15, initial.reshape(1024, 128), state)
    block = pltpu.VMEM((16, 64, 128), F32)
    faces = call(faces_kernel, [face] * 4, 0, 1 << 19, [block], smem=False)(leaving)
    fine_cost = (2 * 64 * 480 * 2048, 3 << 19)
    v = send(leaving, ring(1, 0, 0))
    hops = (ring(1, 1, 0), ring(1, -1, 0), ring(1, 0, 1), ring(1, 0, -1))
    for step in range(3):
        xb, xa, yb, ya = [send(f, pairs) for f, pairs in zip(faces, hops)]
        kernel, held = (fine_kernel, []) if step else (first_fine_kernel, [block])
        v, *faces = call(kernel, [whole] + [face] * 4, *fine_cost, held)(
            flags, v, source, xb, xa, yb, ya, w
        )
        hops = (ring(0, 1, 0), ring(0, -1, 0), ring(0, 0, 1), ring(0, 0, -1))
    xb, xa, yb, ya = [send(f, pairs) for f, pairs in zip(faces, hops)]
    resid, r = call(residual_kernel, [rows, whole], *fine_cost)(
        flags, v, source, xb, xa, yb, ya, w, state
    )

    pieces = r.reshape(16, 64, 64, 2).transpose(2, 3, 1, 0)
    pieces = lax.all_to_all(pieces, ("tj", "sx", "sy"), 0, 0, tiled=True)
    pieces = pieces.reshape(4, 4, 4, 2, 64, 4, 4).transpose(0, 3, 1, 5, 2, 6, 4)
    r = pieces.reshape(16, 128, 64).transpose(0, 2, 1)

    up_ring, down_ring = slab_ring(0, 1), slab_ring(0, -1)

    def exchange(pair):
        up, down = pair
        return send(up, up_ring), send(down, down_ring)

    pair_cost = (2 * 64 * 480 * 1536, 1 << 19)
    scratch = [pltpu.VMEM((8, 64, 128), F32), pltpu.VMEM((8, 64, 128), F32)]
    pair = call(local_first_kernel, [((2, 144, 128), F32)] * 2, 0, 1 << 18, smem=False)(r)
    e, *pair = call(local_pair_kernel, [((12, 64, 128), F32), trace, trace], *pair_cost, scratch)(
        flags, r, *exchange(pair), w
    )
    e3, *pair = call(local_last_kernel, [two, wide, wide], *pair_cost)(
        flags, e, r, *exchange(pair), w
    )
    halo = exchange(pair)
    from_1 = send(e3, slab_ring(-1, 0))
    from_2 = send(e3, slab_ring(-2, 0))
    to_1 = send(e3, slab_ring(1, 0))
    chain = call(chain_kernel, [two, wide, wide], *pair_cost, scratch)
    chain_add = call(chain_add_kernel, [two, wide, wide], *pair_cost, scratch)
    x, *pair = chain(flags, e3, *halo, w)
    e7, *pair = chain_add(flags, x, *exchange(pair), w, from_1)
    halo = exchange(pair)
    to_2 = send(e7, slab_ring(2, 0))
    x, *pair = chain(flags, e7, *halo, w)
    e11, *pair = chain_add(flags, x, *exchange(pair), w, from_2)
    to_3 = send(e11, slab_ring(3, 0))
    x, *pair = call(pick_kernel, [two, wide, wide], 0, 1 << 18)(flags, to_1, to_2, to_3)
    head, x, *pair = call(
        last_first_kernel, [((8, 64, 128), F32), two, wide, wide], *pair_cost, scratch
    )(flags, x, *exchange(pair), w, e)
    (tail,) = call(last_second_kernel, [((8, 64, 128), F32)], *pair_cost, scratch)(
        flags, x, *exchange(pair), w, e, e3
    )
    error = jnp.concatenate([head, tail], 0)

    pieces = error.transpose(0, 2, 1).reshape(4, 2, 4, 4, 4, 4, 64).transpose(0, 2, 4, 1, 6, 3, 5)
    pieces = pieces.reshape(64, 2, 64, 16)
    pieces = lax.all_to_all(pieces, ("tj", "sx", "sy"), 0, 0, tiled=True)
    error = pieces.transpose(2, 3, 0, 1).reshape(1024, 128)
    corrected = state + error
    shape = (1, 64, 4, 4, 128)
    return corrected.reshape(shape), resid.reshape(shape)


def solution(mesh):
    fine = Mesh(mesh.devices.reshape(4, 4, 4, 4), AXES)
    time = ("tg", "tj")
    placed = (
        P(time, None, "sx", "sy", None),
        P(time, None, "sx", "sy", None),
        P(None, "sx", "sy", None),
        P(),
        P(),
    )
    return jax.shard_map(
        local,
        mesh=fine,
        in_specs=placed,
        out_specs=(P(time, None, "sx", "sy", None), P(time, None, "sx", "sy", None)),
        check_vma=False,
    )
```

```python
import functools

import jax
import jax.numpy as jnp
from jax import lax
from jax.experimental import pallas as pl
from jax.experimental.pallas import tpu as pltpu
from jax.sharding import Mesh, PartitionSpec as P

F32, BF16 = jnp.float32, jnp.bfloat16
AXES = ("tg", "tj", "sx", "sy")
FLAG = pl.BlockSpec(memory_space=pltpu.SMEM)
VM = pl.BlockSpec(memory_space=pltpu.VMEM)
PARAMS = pltpu.CompilerParams(vmem_limit_bytes=40 << 20)
XB, XA, YB, YA, ZB, ZA, G0, G1, G2, G3, FIRST, LAST = range(12)


def ring_of_slabs():
    path = []
    for x in range(4):
        path += [(0, x, y if x % 2 == 0 else 3 - y) for y in range(4)]
    path += [(1, x, y) for _, x, y in reversed(path)]
    return [(2 * c + k) * 16 + 4 * x + y for c, x, y in path for k in range(2)]


DEVICE = ring_of_slabs()
SLAB = [DEVICE.index(d) for d in range(64)]


def call(kernel, out, flops, nbytes, scratch=(), smem=True):
    def run(*args):
        specs = [VM] * len(args)
        if smem:
            specs[0] = FLAG
        return pl.pallas_call(
            kernel,
            out_shape=[jax.ShapeDtypeStruct(s, d) for s, d in out],
            in_specs=specs,
            out_specs=[VM] * len(out),
            scratch_shapes=list(scratch),
            compiler_params=PARAMS,
            cost_estimate=pl.CostEstimate(flops=flops, bytes_accessed=nbytes, transcendentals=0),
        )(*args)

    return run


def split(value):
    high = value.astype(BF16)
    return high, (value - high.astype(F32)).astype(BF16)


def weights_kernel(w_ref, o_ref):
    high, low = split(w_ref[...])
    o_ref[:, 0:160] = high
    o_ref[:, 160:320] = high
    o_ref[:, 320:480] = low


def product(w, parts):
    high, low = split(jnp.concatenate(parts, 0))
    return jnp.dot(w, jnp.concatenate([high, low, high], 0), preferred_element_type=F32)


def y_trace(ref, b, t):
    return jnp.concatenate([ref[t, 16 * a + 4 * b : 16 * a + 4 * b + 4, :] for a in range(4)], 0)


def z_trace(ref, c, t):
    return ref[t, pl.ds(c, 16, stride=4), :]


def tiles(ref, rows, which):
    return jnp.concatenate([ref[t, rows, :] for t in which], 1)


def lanes(shape):
    return lax.broadcasted_iota(jnp.int32, shape, 1)


ALL = slice(None)


def given(ref, t):
    return ref[pl.ds(t, 64, stride=16), :]


def emit_faces(ref, xp, xm, yp, ym):
    for i in range(4):
        xp[i] = ref[12 + i, 48:64, :]
        xm[i] = ref[i, 0:16, :]
        yp[i] = y_trace(ref, 3, 4 * i + 3)
        ym[i] = y_trace(ref, 0, 4 * i)


def gather(flags, which, initial, state, held):
    @pl.when(flags[which] == 1.0)
    def _():
        for t in range(16):
            held[t] = given(initial, t)

    @pl.when(flags[which] == 0.0)
    def _():
        for t in range(16):
            held[t] = given(state, t)


def faces_kernel(flags, initial, state, xp, xm, yp, ym, held):
    gather(flags, LAST, initial, state, held)
    emit_faces(held, xp, xm, yp, ym)


def fine_step(flags, v, source, xb, xa, yb, ya, w, store):
    weight = w[...]
    lane = lanes((16, 128))
    for i in range(4):
        row = [4 * i + j for j in range(4)]
        own = tiles(v, ALL, row)
        if i == 0:
            below_x = tiles(xb, ALL, range(4)) * flags[XB]
        else:
            below_x = tiles(v, slice(48, 64), [t - 4 for t in row])
        if i == 3:
            above_x = tiles(xa, ALL, range(4)) * flags[XA]
        else:
            above_x = tiles(v, slice(0, 16), [t + 4 for t in row])
        below_y = jnp.concatenate([yb[i] * flags[YB]] + [y_trace(v, 3, t) for t in row[:3]], 1)
        above_y = jnp.concatenate([y_trace(v, 0, t) for t in row[1:]] + [ya[i] * flags[YA]], 1)
        below_z = [jnp.where(lane == 0, 0.0, pltpu.roll(z_trace(v, 3, t), 1, 1)) for t in row]
        above_z = [jnp.where(lane == 127, 0.0, pltpu.roll(z_trace(v, 0, t), 127, 1)) for t in row]
        mixed = product(
            weight,
            [own, below_x, above_x, below_y, above_y]
            + [jnp.concatenate(below_z, 1), jnp.concatenate(above_z, 1)],
        )
        value = (own - 0.1 * own) + mixed
        for j, t in enumerate(row):
            store(t, value[:, 128 * j : 128 * j + 128] + given(source, t))


def first_fine_kernel(flags, v, source, xb, xa, yb, ya, w, initial, out, xp, xm, yp, ym, held):
    gather(flags, FIRST, initial, v, held)
    fine_kernel(flags, held, source, xb, xa, yb, ya, w, out, xp, xm, yp, ym)


def fine_kernel(flags, v, source, xb, xa, yb, ya, w, out, xp, xm, yp, ym):
    def store(t, value):
        out[t] = value

    fine_step(flags, v, source, xb, xa, yb, ya, w, store)
    emit_faces(out, xp, xm, yp, ym)


def residual_kernel(flags, v, source, xb, xa, yb, ya, w, state, out, packed, held):
    def store(t, value):
        value = value - given(state, t)
        out[pl.ds(t, 64, stride=16), :] = value
        held[t] = value

    fine_step(flags, v, source, xb, xa, yb, ya, w, store)
    for m in range(8):
        value = jnp.concatenate([held[2 * m], held[2 * m + 1]], 0).T
        packed[pl.ds(m, 128, stride=8), :] = value


def corrected_kernel(received, state, out):
    for m in range(8):
        block = received[pl.ds(m, 128, stride=8), :].T
        for low in range(2):
            t = 2 * m + low
            out[pl.ds(t, 64, stride=16), :] = block[64 * low : 64 * low + 64] + given(state, t)


def coarse_plane(weight, ref, p, below_z, above_z):
    even, odd = 2 * p, 2 * p + 1
    own = tiles(ref, ALL, (even, odd))
    lane = lanes((16, 128))
    x_high, y_high, x_low, y_low = lane // 32, lane // 8 % 4, lane // 2 % 4, lane % 2

    def moved(value, near, first, far, edge):
        away = jnp.where(edge, 0.0, pltpu.roll(value, far, 1))
        return jnp.where(first, away, pltpu.roll(value, near, 1))

    low_x, top_x = x_low == 0, x_low == 3
    low_y, top_y = y_low == 0, y_low == 1
    below_x = [moved(ref[t, 48:64, :], 2, low_x, 26, x_high == 0) for t in (even, odd)]
    above_x = [moved(ref[t, 0:16, :], 126, top_x, 102, x_high == 3) for t in (even, odd)]
    below_y = [
        moved(y_trace(ref, 3, odd), 1, low_y, 7, y_high == 0),
        y_trace(ref, 3, even),
    ]
    above_y = [
        y_trace(ref, 0, odd),
        moved(y_trace(ref, 0, even), 127, top_y, 121, y_high == 3),
    ]
    sides = [jnp.concatenate(pair, 1) for pair in (below_x, above_x, below_y, above_y)]
    mixed = product(weight, [own] + sides + [below_z, above_z])
    return (own - 0.4 * own) + 4.0 * mixed


def plane(ref, p):
    return tiles(ref, ALL, (2 * p, 2 * p + 1))


def put(ref, p, value, rows=ALL):
    ref[2 * p, rows, :] = value[:, 0:128]
    ref[2 * p + 1, rows, :] = value[:, 128:256]


def z_plane(ref, c, p):
    return jnp.concatenate([z_trace(ref, c, 2 * p), z_trace(ref, c, 2 * p + 1)], 1)


def emit_wide(ref, up, down):
    put(up, 0, plane(ref, 1), slice(0, 64))
    put(up, 0, z_plane(ref, 3, 0), slice(64, 80))
    put(down, 0, plane(ref, 0), slice(0, 64))
    put(down, 0, z_plane(ref, 0, 1), slice(64, 80))


def pair_steps(flags, v, below, above, w, extended, first, add_first, add_second, add_halo):
    weight = w[...]
    has_below, has_above = flags[ZB], flags[ZA]
    both = (0, 1)
    put(extended, 0, tiles(below, slice(0, 64), both) * has_below)
    put(extended, 1, plane(v, 0))
    put(extended, 2, plane(v, 1))
    put(extended, 3, tiles(above, slice(0, 64), both) * has_above)
    for p in range(4):
        if p == 0:
            lower = tiles(below, slice(64, 80), both) * has_below
        else:
            lower = z_plane(extended, 3, p - 1)
        if p == 3:
            upper = tiles(above, slice(64, 80), both) * has_above
        else:
            upper = z_plane(extended, 0, p + 1)
        value = coarse_plane(weight, extended, p, lower, upper)
        if p == 0:
            if add_halo:
                value = value + tiles(below, slice(80, 144), both)
            value = value * has_below
        elif p == 3:
            if add_halo:
                value = value + tiles(above, slice(80, 144), both)
            value = value * has_above
        elif add_first is not None:
            value = value + add_first(p - 1)
        put(first, p, value)
    result = []
    for p in (1, 2):
        value = coarse_plane(weight, first, p, z_plane(first, 3, p - 1), z_plane(first, 0, p + 1))
        result.append(value if add_second is None else value + add_second(p - 1))
    return result


def local_first_kernel(received, r, up, down):
    for q in range(8):
        at = [SLAB[q // 2 * 16 + s] * 16 + 8 * (q % 2) for s in range(16)]
        block = jnp.concatenate([received[a : a + 8, :] for a in at], 0).T
        r[2 * q] = block[0:64]
        r[2 * q + 1] = block[64:128]
    emit_wide(r, up, down)
    put(up, 0, plane(r, 3), slice(80, 144))
    put(down, 0, plane(r, 2), slice(80, 144))


def local_pair_kernel(flags, r, below, above, w, out, up, down, extended, first):
    result = pair_steps(
        flags, r, below, above, w, extended, first,
        lambda p: plane(r, 2 + p), lambda p: plane(r, 4 + p), True,
    )
    for p in range(2):
        put(out, p, plane(r, p))
        put(out, 2 + p, plane(first, 1 + p))
        put(out, 4 + p, result[p])
    put(up, 0, z_plane(out, 3, 5))
    put(down, 0, z_plane(out, 0, 4))


def local_last_kernel(flags, e, r, below, above, w, out, up, down):
    weight = w[...]
    for p in range(2):
        lower = plane(below, 0) * flags[ZB] if p == 0 else z_plane(e, 3, 4)
        upper = plane(above, 0) * flags[ZA] if p == 1 else z_plane(e, 0, 5)
        put(out, p, coarse_plane(weight, e, 4 + p, lower, upper) + plane(r, 6 + p))
    emit_wide(out, up, down)


def chain_kernel(flags, v, below, above, w, out, up, down, extended, first):
    result = pair_steps(flags, v, below, above, w, extended, first, None, None, False)
    for p in range(2):
        put(out, p, result[p])
    emit_wide(out, up, down)


def chain_add_kernel(flags, v, below, above, w, add, own, out, ship, up, down, extended, first):
    result = pair_steps(
        flags, v, below, above, w, extended, first, None, lambda p: plane(add, p), False
    )
    for p in range(2):
        put(out, p, result[p])
        put(ship, p, result[p] * flags[G0] + plane(own, p) * (1.0 - flags[G0]))
    emit_wide(out, up, down)


def pick_kernel(flags, one, two, three, out, up, down):
    out[...] = one[...] * flags[G1] + two[...] * flags[G2] + three[...] * flags[G3]
    emit_wide(out, up, down)


def last_first_kernel(flags, v, below, above, w, e, out, tail, up, down, extended, first):
    result = pair_steps(flags, v, below, above, w, extended, first, None, None, False)
    for p in range(2):
        put(out, p, plane(first, 1 + p) + plane(e, p))
        put(tail, p, result[p])
        put(out, 2 + p, result[p] + plane(e, 2 + p))
    emit_wide(tail, up, down)


def last_second_kernel(flags, v, below, above, w, e, e3, head, packed, extended, first):
    result = pair_steps(flags, v, below, above, w, extended, first, None, None, False)
    for q in range(8):
        if q < 4:
            block = jnp.concatenate([head[2 * q], head[2 * q + 1]], 0)
        else:
            p = q % 2
            value = plane(first, 1 + p) + plane(e, 4 + p) if q < 6 else result[p] + plane(e3, p)
            block = jnp.concatenate([value[:, 0:128], value[:, 128:256]], 0)
        block = block.T
        for s in range(16):
            at = SLAB[q // 2 * 16 + s] * 16 + 8 * (q % 2)
            packed[at : at + 8, :] = block[8 * s : 8 * s + 8]


def index_of(t, x, y):
    return (t * 4 + x) * 4 + y


def ring(dt, dx, dy):
    return [
        (index_of(t, x, y), index_of((t + dt) % 16, (x + dx) % 4, (y + dy) % 4))
        for t in range(16)
        for x in range(4)
        for y in range(4)
    ]


def slab_ring(ds):
    return [
        (64 * g + DEVICE[s], 64 * g + DEVICE[(s + ds) % 64]) for g in range(4) for s in range(64)
    ]


def group_swap(mask):
    return [(64 * g + s, 64 * (g ^ mask) + s) for g in range(4) for s in range(64)]


def send(value, pairs):
    return lax.ppermute(value, AXES, pairs)


def local(slices_state, forcing, initial, volume, lift):
    tg, tj = lax.axis_index("tg"), lax.axis_index("tj")
    sx, sy = lax.axis_index("sx"), lax.axis_index("sy")
    corner = (sx == 0) & (sy == 0)
    tm = tg * 4 + tj
    flags = jnp.stack(
        [sx > 0, sx < 3, sy > 0, sy < 3, ~(corner & (tj == 0)), ~(corner & (tj == 3))]
        + [tg == 0, tg == 1, tg == 2, tg == 3, tm == 0, tm == 15]
    ).astype(F32)
    lift_flat = jnp.transpose(lift, (1, 0, 2)).reshape(64, 96)
    w = jnp.concatenate([volume, lift_flat], 1)
    face, wide, trace = ((4, 16, 128), F32), ((2, 80, 128), F32), ((2, 16, 128), F32)
    whole, two, rows = ((16, 64, 128), F32), ((4, 64, 128), F32), ((1024, 128), F32)
    (w,) = call(weights_kernel, [((64, 480), BF16)], 0, 1 << 17, smem=False)(w)

    state = slices_state.reshape(1024, 128)
    source = forcing.reshape(1024, 128)
    start = initial.reshape(1024, 128)
    block = pltpu.VMEM((16, 64, 128), F32)
    faces = call(faces_kernel, [face] * 4, 0, 1 << 19, [block])(flags, start, state)
    fine_cost = (2 * 64 * 480 * 2048, 3 << 19)
    v = send(state, ring(1, 0, 0))
    hops = (ring(1, 1, 0), ring(1, -1, 0), ring(1, 0, 1), ring(1, 0, -1))
    for step in range(3):
        xb, xa, yb, ya = [send(f, pairs) for f, pairs in zip(faces, hops)]
        kernel, held, more = (fine_kernel, [], []) if step else (first_fine_kernel, [block], [start])
        v, *faces = call(kernel, [whole] + [face] * 4, *fine_cost, held)(
            flags, v, source, xb, xa, yb, ya, w, *more
        )
        hops = (ring(0, 1, 0), ring(0, -1, 0), ring(0, 0, 1), ring(0, 0, -1))
    xb, xa, yb, ya = [send(f, pairs) for f, pairs in zip(faces, hops)]
    resid, packed = call(residual_kernel, [rows, rows], *fine_cost, [block])(
        flags, v, source, xb, xa, yb, ya, w, state
    )

    peers = [[64 * g + d for d in DEVICE] for g in range(4)]

    def traded(value):
        return lax.all_to_all(value, AXES, 0, 0, axis_index_groups=peers, tiled=True)

    received = traded(packed)

    up_ring, down_ring = slab_ring(1), slab_ring(-1)

    def exchange(pair):
        up, down = pair
        return send(up, up_ring), send(down, down_ring)

    pair_cost = (2 * 64 * 480 * 1536, 1 << 19)
    scratch = [pltpu.VMEM((8, 64, 128), F32), pltpu.VMEM((8, 64, 128), F32)]
    r, *pair = call(
        local_first_kernel, [whole] + [((2, 144, 128), F32)] * 2, 0, 1 << 20, smem=False
    )(received)
    e, *pair = call(local_pair_kernel, [((12, 64, 128), F32), trace, trace], *pair_cost, scratch)(
        flags, r, *exchange(pair), w
    )
    e3, *pair = call(local_last_kernel, [two, wide, wide], *pair_cost)(
        flags, e, r, *exchange(pair), w
    )
    halo = exchange(pair)
    swap_1 = send(e3, group_swap(1))
    chain = call(chain_kernel, [two, wide, wide], *pair_cost, scratch)
    chain_add = call(chain_add_kernel, [two, two, wide, wide], *pair_cost, scratch)
    x, *pair = chain(flags, e3, *halo, w)
    e7, ship, *pair = chain_add(flags, x, *exchange(pair), w, swap_1, e3)
    halo = exchange(pair)
    swap_2 = send(ship, group_swap(2))
    x, *pair = chain(flags, e7, *halo, w)
    e11, ship, *pair = chain_add(flags, x, *exchange(pair), w, swap_2, e3)
    swap_3 = send(ship, group_swap(3))
    x, *pair = call(pick_kernel, [two, wide, wide], 0, 1 << 18)(flags, swap_1, swap_2, swap_3)
    head, x, *pair = call(
        last_first_kernel, [((8, 64, 128), F32), two, wide, wide], *pair_cost, scratch
    )(flags, x, *exchange(pair), w, e)
    (packed,) = call(last_second_kernel, [rows], *pair_cost, scratch)(
        flags, x, *exchange(pair), w, e, e3, head
    )
    received = traded(packed)
    (corrected,) = call(corrected_kernel, [rows], 0, 3 << 19, smem=False)(received, state)
    shape = (1, 64, 4, 4, 128)
    return corrected.reshape(shape), resid.reshape(shape)


def solution(mesh):
    fine = Mesh(mesh.devices.reshape(4, 4, 4, 4), AXES)
    time = ("tg", "tj")
    placed = (
        P(time, None, "sx", "sy", None),
        P(time, None, "sx", "sy", None),
        P(None, "sx", "sy", None),
        P(),
        P(),
    )
    return jax.shard_map(
        local,
        mesh=fine,
        in_specs=placed,
        out_specs=(P(time, None, "sx", "sy", None), P(time, None, "sx", "sy", None)),
        check_vma=False,
    )
```

```python
import functools

import jax
import jax.numpy as jnp
from jax import lax
from jax.experimental import pallas as pl
from jax.experimental.pallas import tpu as pltpu
from jax.sharding import Mesh, PartitionSpec as P

F32, BF16 = jnp.float32, jnp.bfloat16
AXES = ("tg", "tj", "sx", "sy")
VM = pl.BlockSpec(memory_space=pltpu.VMEM)
ANY = pl.BlockSpec(memory_space=pl.ANY)
PARAMS = pltpu.CompilerParams(vmem_limit_bytes=40 << 20)
XB, XA, YB, YA, ZB, ZA, FROM_1, FROM_2, FROM_3, FIRST, LAST = range(11)


def ring_of_slabs():
    path = []
    for x in range(4):
        path += [(0, x, y if x % 2 == 0 else 3 - y) for y in range(4)]
    path += [(1, x, y) for _, x, y in reversed(path)]
    return [(2 * c + k) * 16 + 4 * x + y for c, x, y in path for k in range(2)]


DEVICE = ring_of_slabs()
SLAB = [DEVICE.index(d) for d in range(64)]


def call(kernel, out, flops, nbytes, scratch=(), specs=None):
    def run(*args):
        return pl.pallas_call(
            kernel,
            out_shape=[jax.ShapeDtypeStruct(s, d) for s, d in out],
            in_specs=specs or [VM] * len(args),
            out_specs=[VM] * len(out),
            scratch_shapes=list(scratch),
            compiler_params=PARAMS,
            cost_estimate=pl.CostEstimate(flops=flops, bytes_accessed=nbytes, transcendentals=0),
        )(*args)

    return run


def split(value):
    high = value.astype(BF16)
    return high, (value - high.astype(F32)).astype(BF16)


def weights_kernel(w_ref, o_ref):
    high, low = split(w_ref[...])
    o_ref[:, 0:160] = high
    o_ref[:, 160:320] = high
    o_ref[:, 320:480] = low


def product(w, parts):
    high, low = split(jnp.concatenate(parts, 0))
    return jnp.dot(w, jnp.concatenate([high, low, high], 0), preferred_element_type=F32)


def y_trace(ref, b, t):
    return jnp.concatenate([ref[t, 16 * a + 4 * b : 16 * a + 4 * b + 4, :] for a in range(4)], 0)


def z_trace(ref, c, t):
    return ref[t, pl.ds(c, 16, stride=4), :]


def tiles(ref, rows, which):
    return jnp.concatenate([ref[t, rows, :] for t in which], 1)


def flag(flags, which, wide=1):
    return jnp.concatenate([flags[which : which + 1, :]] * wide, 1)


def lanes(shape):
    return lax.broadcasted_iota(jnp.int32, shape, 1)


ALL = slice(None)


def given(ref, t):
    return ref[pl.ds(t, 64, stride=16), :]


def emit_faces(ref, xp, xm, yp, ym):
    for i in range(4):
        xp[i] = ref[12 + i, 48:64, :]
        xm[i] = ref[i, 0:16, :]
        yp[i] = y_trace(ref, 3, 4 * i + 3)
        ym[i] = y_trace(ref, 0, 4 * i)


def gather(flags, which, initial, state, held):
    chosen = flag(flags, which) > 0.5
    for t in range(16):
        held[t] = jnp.where(chosen, given(initial, t), given(state, t))


def faces_kernel(flags, initial, state, xp, xm, yp, ym, held):
    gather(flags, LAST, initial, state, held)
    emit_faces(held, xp, xm, yp, ym)


def fine_step(flags, v, source, xb, xa, yb, ya, w, store):
    weight = w[...]
    lane = lanes((16, 128))
    for i in range(4):
        row = [4 * i + j for j in range(4)]
        own = tiles(v, ALL, row)
        if i == 0:
            below_x = tiles(xb, ALL, range(4)) * flag(flags, XB, 4)
        else:
            below_x = tiles(v, slice(48, 64), [t - 4 for t in row])
        if i == 3:
            above_x = tiles(xa, ALL, range(4)) * flag(flags, XA, 4)
        else:
            above_x = tiles(v, slice(0, 16), [t + 4 for t in row])
        below_y = jnp.concatenate([yb[i] * flag(flags, YB)] + [y_trace(v, 3, t) for t in row[:3]], 1)
        above_y = jnp.concatenate([y_trace(v, 0, t) for t in row[1:]] + [ya[i] * flag(flags, YA)], 1)
        below_z = [jnp.where(lane == 0, 0.0, pltpu.roll(z_trace(v, 3, t), 1, 1)) for t in row]
        above_z = [jnp.where(lane == 127, 0.0, pltpu.roll(z_trace(v, 0, t), 127, 1)) for t in row]
        mixed = product(
            weight,
            [own, below_x, above_x, below_y, above_y]
            + [jnp.concatenate(below_z, 1), jnp.concatenate(above_z, 1)],
        )
        value = (own - 0.1 * own) + mixed
        for j, t in enumerate(row):
            store(t, value[:, 128 * j : 128 * j + 128] + given(source, t))


def first_fine_kernel(flags, v, source, xb, xa, yb, ya, w, initial, out, xp, xm, yp, ym, held):
    gather(flags, FIRST, initial, v, held)
    fine_kernel(flags, held, source, xb, xa, yb, ya, w, out, xp, xm, yp, ym)


def fine_kernel(flags, v, source, xb, xa, yb, ya, w, out, xp, xm, yp, ym):
    def store(t, value):
        out[t] = value

    fine_step(flags, v, source, xb, xa, yb, ya, w, store)
    emit_faces(out, xp, xm, yp, ym)


def residual_kernel(flags, v, source, xb, xa, yb, ya, w, state, out, packed, held):
    def store(t, value):
        value = value - given(state, t)
        out[pl.ds(t, 64, stride=16), :] = value
        held[t] = value

    fine_step(flags, v, source, xb, xa, yb, ya, w, store)
    for m in range(8):
        value = jnp.concatenate([held[2 * m], held[2 * m + 1]], 0).T
        packed[pl.ds(m, 128, stride=8), :] = value


def corrected_kernel(received, state, out):
    for m in range(8):
        block = received[pl.ds(m, 128, stride=8), :].T
        for low in range(2):
            t = 2 * m + low
            out[pl.ds(t, 64, stride=16), :] = block[64 * low : 64 * low + 64] + given(state, t)


def coarse_plane(weight, ref, p, below_z, above_z):
    even, odd = 2 * p, 2 * p + 1
    own = tiles(ref, ALL, (even, odd))
    lane = lanes((16, 128))
    x_high, y_high, x_low, y_low = lane // 32, lane // 8 % 4, lane // 2 % 4, lane % 2

    def moved(value, near, first, far, edge):
        away = jnp.where(edge, 0.0, pltpu.roll(value, far, 1))
        return jnp.where(first, away, pltpu.roll(value, near, 1))

    low_x, top_x = x_low == 0, x_low == 3
    low_y, top_y = y_low == 0, y_low == 1
    below_x = [moved(ref[t, 48:64, :], 2, low_x, 26, x_high == 0) for t in (even, odd)]
    above_x = [moved(ref[t, 0:16, :], 126, top_x, 102, x_high == 3) for t in (even, odd)]
    below_y = [
        moved(y_trace(ref, 3, odd), 1, low_y, 7, y_high == 0),
        y_trace(ref, 3, even),
    ]
    above_y = [
        y_trace(ref, 0, odd),
        moved(y_trace(ref, 0, even), 127, top_y, 121, y_high == 3),
    ]
    sides = [jnp.concatenate(pair, 1) for pair in (below_x, above_x, below_y, above_y)]
    mixed = product(weight, [own] + sides + [below_z, above_z])
    return (own - 0.4 * own) + 4.0 * mixed


def plane(ref, p):
    return tiles(ref, ALL, (2 * p, 2 * p + 1))


def put(ref, p, value, rows=ALL):
    ref[2 * p, rows, :] = value[:, 0:128]
    ref[2 * p + 1, rows, :] = value[:, 128:256]


def z_plane(ref, c, p):
    return jnp.concatenate([z_trace(ref, c, 2 * p), z_trace(ref, c, 2 * p + 1)], 1)


def emit_wide(ref, up, down):
    put(up, 0, plane(ref, 1), slice(0, 64))
    put(up, 0, z_plane(ref, 3, 0), slice(64, 80))
    put(down, 0, plane(ref, 0), slice(0, 64))
    put(down, 0, z_plane(ref, 0, 1), slice(64, 80))


def pair_steps(flags, v, below, above, w, extended, first, add_first, add_second, add_halo):
    weight = w[...]
    has_below, has_above = flag(flags, ZB, 2), flag(flags, ZA, 2)
    both = (0, 1)
    put(extended, 0, tiles(below, slice(0, 64), both) * has_below)
    put(extended, 1, plane(v, 0))
    put(extended, 2, plane(v, 1))
    put(extended, 3, tiles(above, slice(0, 64), both) * has_above)
    for p in range(4):
        if p == 0:
            lower = tiles(below, slice(64, 80), both) * has_below
        else:
            lower = z_plane(extended, 3, p - 1)
        if p == 3:
            upper = tiles(above, slice(64, 80), both) * has_above
        else:
            upper = z_plane(extended, 0, p + 1)
        value = coarse_plane(weight, extended, p, lower, upper)
        if p == 0:
            if add_halo:
                value = value + tiles(below, slice(80, 144), both)
            value = value * has_below
        elif p == 3:
            if add_halo:
                value = value + tiles(above, slice(80, 144), both)
            value = value * has_above
        elif add_first is not None:
            value = value + add_first(p - 1)
        put(first, p, value)
    result = []
    for p in (1, 2):
        value = coarse_plane(weight, first, p, z_plane(first, 3, p - 1), z_plane(first, 0, p + 1))
        result.append(value if add_second is None else value + add_second(p - 1))
    return result


def local_first_kernel(received, r, up, down):
    for q in range(8):
        at = [SLAB[q // 2 * 16 + s] * 16 + 8 * (q % 2) for s in range(16)]
        block = jnp.concatenate([received[a : a + 8, :] for a in at], 0).T
        r[2 * q] = block[0:64]
        r[2 * q + 1] = block[64:128]
    emit_wide(r, up, down)
    put(up, 0, plane(r, 3), slice(80, 144))
    put(down, 0, plane(r, 2), slice(80, 144))


def local_pair_kernel(flags, r, below, above, w, out, up, down, extended, first):
    result = pair_steps(
        flags, r, below, above, w, extended, first,
        lambda p: plane(r, 2 + p), lambda p: plane(r, 4 + p), True,
    )
    for p in range(2):
        put(out, p, plane(r, p))
        put(out, 2 + p, plane(first, 1 + p))
        put(out, 4 + p, result[p])
    put(up, 0, z_plane(out, 3, 5))
    put(down, 0, z_plane(out, 0, 4))


def local_last_kernel(flags, e, r, below, above, w, out):
    weight = w[...]
    for p in range(2):
        lower = plane(below, 0) * flag(flags, ZB, 2) if p == 0 else z_plane(e, 3, 4)
        upper = plane(above, 0) * flag(flags, ZA, 2) if p == 1 else z_plane(e, 0, 5)
        put(out, p, coarse_plane(weight, e, 4 + p, lower, upper) + plane(r, 6 + p))


def chain_kernel(flags, v, below, above, w, out, up, down, extended, first):
    result = pair_steps(flags, v, below, above, w, extended, first, None, None, False)
    for p in range(2):
        put(out, p, result[p])
    emit_wide(out, up, down)


def chain_add_kernel(which, flags, v, below, above, w, add, out, up, down, extended, first):
    chosen = flag(flags, which, 2) > 0.5
    result = pair_steps(
        flags, v, below, above, w, extended, first, None,
        lambda p: jnp.where(chosen, plane(add, p), 0.0), False,
    )
    for p in range(2):
        put(out, p, result[p])
    emit_wide(out, up, down)


def begin_kernel(flags, v, waited, out, up, down):
    for t in range(4):
        out[t] = jnp.where(flag(flags, FROM_3) > 0.5, v[t], 0.0)
    emit_wide(out, up, down)


def last_first_kernel(flags, v, below, above, w, e, out, tail, up, down, extended, first):
    result = pair_steps(flags, v, below, above, w, extended, first, None, None, False)
    for p in range(2):
        put(out, p, plane(first, 1 + p) + plane(e, p))
        put(tail, p, result[p])
        put(out, 2 + p, result[p] + plane(e, 2 + p))
    emit_wide(tail, up, down)


def last_second_kernel(flags, v, below, above, w, e, e3, head, packed, extended, first):
    result = pair_steps(flags, v, below, above, w, extended, first, None, None, False)
    for q in range(8):
        if q < 4:
            block = jnp.concatenate([head[2 * q], head[2 * q + 1]], 0)
        else:
            p = q % 2
            value = plane(first, 1 + p) + plane(e, 4 + p) if q < 6 else result[p] + plane(e3, p)
            block = jnp.concatenate([value[:, 0:128], value[:, 128:256]], 0)
        block = block.T
        for s in range(16):
            at = SLAB[q // 2 * 16 + s] * 16 + 8 * (q % 2)
            packed[at : at + 8, :] = block[8 * s : 8 * s + 8]


def index_of(t, x, y):
    return (t * 4 + x) * 4 + y


def ring(dt, dx, dy):
    return [
        (index_of(t, x, y), index_of((t + dt) % 16, (x + dx) % 4, (y + dy) % 4))
        for t in range(16)
        for x in range(4)
        for y in range(4)
    ]


def slab_ring(ds, dg=0):
    return [
        (64 * g + DEVICE[s], 64 * ((g + dg) % 4) + DEVICE[(s + ds) % 64])
        for g in range(4)
        for s in range(64)
    ]


def send(value, pairs):
    return lax.ppermute(value, AXES, pairs)


def local(slices_state, forcing, initial, volume, lift):
    tg, tj = lax.axis_index("tg"), lax.axis_index("tj")
    sx, sy = lax.axis_index("sx"), lax.axis_index("sy")
    corner = (sx == 0) & (sy == 0)
    tm = tg * 4 + tj
    flags = jnp.stack(
        [sx > 0, sx < 3, sy > 0, sy < 3, ~(corner & (tj == 0)), ~(corner & (tj == 3))]
        + [tg >= 1, tg >= 2, tg >= 3, tm == 0, tm == 15]
    ).astype(F32)
    flags = jnp.broadcast_to(flags[:, None], (11, 128))
    lift_flat = jnp.transpose(lift, (1, 0, 2)).reshape(64, 96)
    w = jnp.concatenate([volume, lift_flat], 1)
    face, wide, trace = ((4, 16, 128), F32), ((2, 80, 128), F32), ((2, 16, 128), F32)
    whole, two, rows = ((16, 64, 128), F32), ((4, 64, 128), F32), ((1024, 128), F32)
    (w,) = call(weights_kernel, [((64, 480), BF16)], 0, 1 << 17)(w)

    state = slices_state.reshape(1024, 128)
    source = forcing.reshape(1024, 128)
    start = initial.reshape(1024, 128)
    block = pltpu.VMEM((16, 64, 128), F32)
    faces = call(faces_kernel, [face] * 4, 0, 1 << 19, [block])(flags, start, state)
    fine_cost = (2 * 64 * 480 * 2048, 3 << 19)
    v = send(state, ring(1, 0, 0))
    hops = (ring(1, 1, 0), ring(1, -1, 0), ring(1, 0, 1), ring(1, 0, -1))
    for step in range(3):
        xb, xa, yb, ya = [send(f, pairs) for f, pairs in zip(faces, hops)]
        kernel, held, more = (fine_kernel, [], []) if step else (first_fine_kernel, [block], [start])
        v, *faces = call(kernel, [whole] + [face] * 4, *fine_cost, held)(
            flags, v, source, xb, xa, yb, ya, w, *more
        )
        hops = (ring(0, 1, 0), ring(0, -1, 0), ring(0, 0, 1), ring(0, 0, -1))
    xb, xa, yb, ya = [send(f, pairs) for f, pairs in zip(faces, hops)]
    resid, packed = call(residual_kernel, [rows, rows], *fine_cost, [block])(
        flags, v, source, xb, xa, yb, ya, w, state
    )

    peers = [[64 * g + d for d in DEVICE] for g in range(4)]

    def traded(value):
        return lax.all_to_all(value, AXES, 0, 0, axis_index_groups=peers, tiled=True)

    received = traded(packed)

    up_ring, down_ring = slab_ring(1), slab_ring(-1)

    def exchange(pair):
        up, down = pair
        return send(up, up_ring), send(down, down_ring)

    pair_cost = (2 * 64 * 480 * 1536, 1 << 19)
    scratch = [pltpu.VMEM((8, 64, 128), F32), pltpu.VMEM((8, 64, 128), F32)]
    r, *pair = call(
        local_first_kernel, [whole] + [((2, 144, 128), F32)] * 2, 0, 1 << 20
    )(received)
    e, *pair = call(local_pair_kernel, [((12, 64, 128), F32), trace, trace], *pair_cost, scratch)(
        flags, r, *exchange(pair), w
    )
    (e3,) = call(local_last_kernel, [two], *pair_cost)(flags, e, r, *exchange(pair), w)
    from_3 = send(e3, slab_ring(0, 3))
    from_1 = send(e3, slab_ring(0, 1))
    chain = call(chain_kernel, [two, wide, wide], *pair_cost, scratch)
    begin = call(begin_kernel, [two, wide, wide], 0, 1 << 18, (), [VM, VM, ANY])
    x, *pair = begin(flags, from_3, from_1)
    from_2 = send(from_1, slab_ring(0, 1))
    for which, add in ((FROM_2, from_2), (FROM_1, from_1)):
        x, *pair = chain(flags, x, *exchange(pair), w)
        kernel = functools.partial(chain_add_kernel, which)
        x, *pair = call(kernel, [two, wide, wide], *pair_cost, scratch)(
            flags, x, *exchange(pair), w, add
        )
    head, x, *pair = call(
        last_first_kernel, [((8, 64, 128), F32), two, wide, wide], *pair_cost, scratch
    )(flags, x, *exchange(pair), w, e)
    (packed,) = call(last_second_kernel, [rows], *pair_cost, scratch)(
        flags, x, *exchange(pair), w, e, e3, head
    )
    received = traded(packed)
    (corrected,) = call(corrected_kernel, [rows], 0, 3 << 19)(received, state)
    shape = (1, 64, 4, 4, 128)
    return corrected.reshape(shape), resid.reshape(shape)


def solution(mesh):
    fine = Mesh(mesh.devices.reshape(4, 4, 4, 4), AXES)
    time = ("tg", "tj")
    placed = (
        P(time, None, "sx", "sy", None),
        P(time, None, "sx", "sy", None),
        P(None, "sx", "sy", None),
        P(),
        P(),
    )
    return jax.shard_map(
        local,
        mesh=fine,
        in_specs=placed,
        out_specs=(P(time, None, "sx", "sy", None), P(time, None, "sx", "sy", None)),
        check_vma=False,
    )
```

```python
import functools

import jax
import jax.numpy as jnp
from jax import lax
from jax.experimental import pallas as pl
from jax.experimental.pallas import tpu as pltpu
from jax.sharding import Mesh, PartitionSpec as P

F32, BF16 = jnp.float32, jnp.bfloat16
AXES = ("tg", "tj", "sx", "sy")
VM = pl.BlockSpec(memory_space=pltpu.VMEM)
ANY = pl.BlockSpec(memory_space=pl.ANY)
PARAMS = pltpu.CompilerParams(vmem_limit_bytes=40 << 20)
XB, XA, YB, YA, ZB, ZA, FROM_1, FROM_2, FROM_3, FIRST, LAST, EX, EY, EZ = range(14)


def ring_of_slabs():
    path = []
    for x in range(4):
        path += [(0, x, y if x % 2 == 0 else 3 - y) for y in range(4)]
    path += [(1, x, y) for _, x, y in reversed(path)]
    return [(2 * c + k) * 16 + 4 * x + y for c, x, y in path for k in range(2)]


DEVICE = ring_of_slabs()
SLAB = [DEVICE.index(d) for d in range(64)]


def call(kernel, out, flops, nbytes, scratch=(), specs=None, ins=(), outs=()):
    def run(*args):
        extra = [pltpu.VMEM(args[i].shape, F32) for i, j, _ in ins for _ in range(2)]
        extra += [pltpu.VMEM(out[i][0], F32) for i, j, _ in outs for _ in range(2)]

        def body(*refs):
            inner = list(refs[: len(args)])
            outer = list(refs[len(args) : len(args) + len(out)])
            own = refs[len(args) + len(out) : len(args) + len(out) + len(scratch)]
            spare = list(refs[len(args) + len(out) + len(scratch) :])
            flags = inner[0]
            sent = []
            for i, j, row in ins:
                first, second = inner[i], inner[j]
                inner[i], inner[j] = spare.pop(0), spare.pop(0)
                even = flags[row : row + 1, :] > 0.5
                for t in range(first.shape[0]):
                    inner[i][t] = jnp.where(even, second[t], first[t])
                    inner[j][t] = jnp.where(even, first[t], second[t])
            for i, j, row in outs:
                up, down = spare.pop(0), spare.pop(0)
                sent.append((outer[i], outer[j], up, down, row))
                outer[i], outer[j] = up, down
            kernel(*inner, *outer, *own)
            for first, second, up, down, row in sent:
                even = flags[row : row + 1, :] > 0.5
                for t in range(first.shape[0]):
                    first[t] = jnp.where(even, up[t], down[t])
                    second[t] = jnp.where(even, down[t], up[t])

        return pl.pallas_call(
            body,
            out_shape=[jax.ShapeDtypeStruct(s, d) for s, d in out],
            in_specs=specs or [VM] * len(args),
            out_specs=[VM] * len(out),
            scratch_shapes=list(scratch) + extra,
            compiler_params=PARAMS,
            cost_estimate=pl.CostEstimate(flops=flops, bytes_accessed=nbytes, transcendentals=0),
        )(*args)

    return run


def split(value):
    high = value.astype(BF16)
    return high, (value - high.astype(F32)).astype(BF16)


def weights_kernel(w_ref, o_ref):
    high, low = split(w_ref[...])
    o_ref[:, 0:160] = high
    o_ref[:, 160:320] = high
    o_ref[:, 320:480] = low


def product(w, parts):
    high, low = split(jnp.concatenate(parts, 0))
    return jnp.dot(w, jnp.concatenate([high, low, high], 0), preferred_element_type=F32)


def y_trace(ref, b, t):
    return jnp.concatenate([ref[t, 16 * a + 4 * b : 16 * a + 4 * b + 4, :] for a in range(4)], 0)


def z_trace(ref, c, t):
    return ref[t, pl.ds(c, 16, stride=4), :]


def tiles(ref, rows, which):
    return jnp.concatenate([ref[t, rows, :] for t in which], 1)


def flag(flags, which, wide=1):
    return jnp.concatenate([flags[which : which + 1, :]] * wide, 1)


def lanes(shape):
    return lax.broadcasted_iota(jnp.int32, shape, 1)


ALL = slice(None)


def given(ref, t):
    return ref[pl.ds(t, 64, stride=16), :]


def emit_faces(ref, xp, xm, yp, ym):
    for i in range(4):
        xp[i] = ref[12 + i, 48:64, :]
        xm[i] = ref[i, 0:16, :]
        yp[i] = y_trace(ref, 3, 4 * i + 3)
        ym[i] = y_trace(ref, 0, 4 * i)


def gather(flags, which, initial, state, held):
    chosen = flag(flags, which) > 0.5
    for t in range(16):
        held[t] = jnp.where(chosen, given(initial, t), given(state, t))


def faces_kernel(flags, initial, state, xp, xm, yp, ym, held):
    gather(flags, LAST, initial, state, held)
    emit_faces(held, xp, xm, yp, ym)


def fine_step(flags, v, source, xb, xa, yb, ya, w, store):
    weight = w[...]
    lane = lanes((16, 128))
    for i in range(4):
        row = [4 * i + j for j in range(4)]
        own = tiles(v, ALL, row)
        if i == 0:
            below_x = tiles(xb, ALL, range(4)) * flag(flags, XB, 4)
        else:
            below_x = tiles(v, slice(48, 64), [t - 4 for t in row])
        if i == 3:
            above_x = tiles(xa, ALL, range(4)) * flag(flags, XA, 4)
        else:
            above_x = tiles(v, slice(0, 16), [t + 4 for t in row])
        below_y = jnp.concatenate([yb[i] * flag(flags, YB)] + [y_trace(v, 3, t) for t in row[:3]], 1)
        above_y = jnp.concatenate([y_trace(v, 0, t) for t in row[1:]] + [ya[i] * flag(flags, YA)], 1)
        below_z = [jnp.where(lane == 0, 0.0, pltpu.roll(z_trace(v, 3, t), 1, 1)) for t in row]
        above_z = [jnp.where(lane == 127, 0.0, pltpu.roll(z_trace(v, 0, t), 127, 1)) for t in row]
        mixed = product(
            weight,
            [own, below_x, above_x, below_y, above_y]
            + [jnp.concatenate(below_z, 1), jnp.concatenate(above_z, 1)],
        )
        value = (own - 0.1 * own) + mixed
        for j, t in enumerate(row):
            store(t, value[:, 128 * j : 128 * j + 128] + given(source, t))


def first_fine_kernel(flags, v, source, xb, xa, yb, ya, w, initial, out, xp, xm, yp, ym, held):
    gather(flags, FIRST, initial, v, held)
    fine_kernel(flags, held, source, xb, xa, yb, ya, w, out, xp, xm, yp, ym)


def fine_kernel(flags, v, source, xb, xa, yb, ya, w, out, xp, xm, yp, ym):
    def store(t, value):
        out[t] = value

    fine_step(flags, v, source, xb, xa, yb, ya, w, store)
    emit_faces(out, xp, xm, yp, ym)


def residual_kernel(flags, v, source, xb, xa, yb, ya, w, state, out, packed, held):
    def store(t, value):
        value = value - given(state, t)
        out[pl.ds(t, 64, stride=16), :] = value
        held[t] = value

    fine_step(flags, v, source, xb, xa, yb, ya, w, store)
    for m in range(8):
        value = jnp.concatenate([held[2 * m], held[2 * m + 1]], 0).T
        packed[pl.ds(m, 128, stride=8), :] = value


def corrected_kernel(received, state, out):
    for m in range(8):
        block = received[pl.ds(m, 128, stride=8), :].T
        for low in range(2):
            t = 2 * m + low
            out[pl.ds(t, 64, stride=16), :] = block[64 * low : 64 * low + 64] + given(state, t)


def coarse_plane(weight, ref, p, below_z, above_z):
    even, odd = 2 * p, 2 * p + 1
    own = tiles(ref, ALL, (even, odd))
    lane = lanes((16, 128))
    x_high, y_high, x_low, y_low = lane // 32, lane // 8 % 4, lane // 2 % 4, lane % 2

    def moved(value, near, first, far, edge):
        away = jnp.where(edge, 0.0, pltpu.roll(value, far, 1))
        return jnp.where(first, away, pltpu.roll(value, near, 1))

    low_x, top_x = x_low == 0, x_low == 3
    low_y, top_y = y_low == 0, y_low == 1
    below_x = [moved(ref[t, 48:64, :], 2, low_x, 26, x_high == 0) for t in (even, odd)]
    above_x = [moved(ref[t, 0:16, :], 126, top_x, 102, x_high == 3) for t in (even, odd)]
    below_y = [
        moved(y_trace(ref, 3, odd), 1, low_y, 7, y_high == 0),
        y_trace(ref, 3, even),
    ]
    above_y = [
        y_trace(ref, 0, odd),
        moved(y_trace(ref, 0, even), 127, top_y, 121, y_high == 3),
    ]
    sides = [jnp.concatenate(pair, 1) for pair in (below_x, above_x, below_y, above_y)]
    mixed = product(weight, [own] + sides + [below_z, above_z])
    return (own - 0.4 * own) + 4.0 * mixed


def plane(ref, p):
    return tiles(ref, ALL, (2 * p, 2 * p + 1))


def put(ref, p, value, rows=ALL):
    ref[2 * p, rows, :] = value[:, 0:128]
    ref[2 * p + 1, rows, :] = value[:, 128:256]


def z_plane(ref, c, p):
    return jnp.concatenate([z_trace(ref, c, 2 * p), z_trace(ref, c, 2 * p + 1)], 1)


def emit_wide(ref, up, down):
    put(up, 0, plane(ref, 1), slice(0, 64))
    put(up, 0, z_plane(ref, 3, 0), slice(64, 80))
    put(down, 0, plane(ref, 0), slice(0, 64))
    put(down, 0, z_plane(ref, 0, 1), slice(64, 80))


def pair_steps(flags, v, below, above, w, extended, first, add_first, add_second, add_halo):
    weight = w[...]
    has_below, has_above = flag(flags, ZB, 2), flag(flags, ZA, 2)
    both = (0, 1)
    put(extended, 0, tiles(below, slice(0, 64), both) * has_below)
    put(extended, 1, plane(v, 0))
    put(extended, 2, plane(v, 1))
    put(extended, 3, tiles(above, slice(0, 64), both) * has_above)
    for p in range(4):
        if p == 0:
            lower = tiles(below, slice(64, 80), both) * has_below
        else:
            lower = z_plane(extended, 3, p - 1)
        if p == 3:
            upper = tiles(above, slice(64, 80), both) * has_above
        else:
            upper = z_plane(extended, 0, p + 1)
        value = coarse_plane(weight, extended, p, lower, upper)
        if p == 0:
            if add_halo:
                value = value + tiles(below, slice(80, 144), both)
            value = value * has_below
        elif p == 3:
            if add_halo:
                value = value + tiles(above, slice(80, 144), both)
            value = value * has_above
        elif add_first is not None:
            value = value + add_first(p - 1)
        put(first, p, value)
    result = []
    for p in (1, 2):
        value = coarse_plane(weight, first, p, z_plane(first, 3, p - 1), z_plane(first, 0, p + 1))
        result.append(value if add_second is None else value + add_second(p - 1))
    return result


def local_first_kernel(flags, received, r, up, down):
    for q in range(8):
        at = [SLAB[q // 2 * 16 + s] * 16 + 8 * (q % 2) for s in range(16)]
        block = jnp.concatenate([received[a : a + 8, :] for a in at], 0).T
        r[2 * q] = block[0:64]
        r[2 * q + 1] = block[64:128]
    emit_wide(r, up, down)
    put(up, 0, plane(r, 3), slice(80, 144))
    put(down, 0, plane(r, 2), slice(80, 144))


def local_pair_kernel(flags, r, below, above, w, out, up, down, extended, first):
    result = pair_steps(
        flags, r, below, above, w, extended, first,
        lambda p: plane(r, 2 + p), lambda p: plane(r, 4 + p), True,
    )
    for p in range(2):
        put(out, p, plane(r, p))
        put(out, 2 + p, plane(first, 1 + p))
        put(out, 4 + p, result[p])
    put(up, 0, z_plane(out, 3, 5))
    put(down, 0, z_plane(out, 0, 4))


def local_last_kernel(flags, e, r, below, above, w, out):
    weight = w[...]
    for p in range(2):
        lower = plane(below, 0) * flag(flags, ZB, 2) if p == 0 else z_plane(e, 3, 4)
        upper = plane(above, 0) * flag(flags, ZA, 2) if p == 1 else z_plane(e, 0, 5)
        put(out, p, coarse_plane(weight, e, 4 + p, lower, upper) + plane(r, 6 + p))


def chain_kernel(flags, v, below, above, w, out, up, down, extended, first):
    result = pair_steps(flags, v, below, above, w, extended, first, None, None, False)
    for p in range(2):
        put(out, p, result[p])
    emit_wide(out, up, down)


def chain_add_kernel(which, flags, v, below, above, w, add, out, up, down, extended, first):
    chosen = flag(flags, which, 2) > 0.5
    result = pair_steps(
        flags, v, below, above, w, extended, first, None,
        lambda p: jnp.where(chosen, plane(add, p), 0.0), False,
    )
    for p in range(2):
        put(out, p, result[p])
    emit_wide(out, up, down)


def begin_kernel(flags, v, waited, out, up, down):
    for t in range(4):
        out[t] = jnp.where(flag(flags, FROM_3) > 0.5, v[t], 0.0)
    emit_wide(out, up, down)


def last_first_kernel(flags, v, below, above, w, e, out, tail, up, down, extended, first):
    result = pair_steps(flags, v, below, above, w, extended, first, None, None, False)
    for p in range(2):
        put(out, p, plane(first, 1 + p) + plane(e, p))
        put(tail, p, result[p])
        put(out, 2 + p, result[p] + plane(e, 2 + p))
    emit_wide(tail, up, down)


def last_second_kernel(flags, v, below, above, w, e, e3, head, packed, extended, first):
    result = pair_steps(flags, v, below, above, w, extended, first, None, None, False)
    for q in range(8):
        if q < 4:
            block = jnp.concatenate([head[2 * q], head[2 * q + 1]], 0)
        else:
            p = q % 2
            value = plane(first, 1 + p) + plane(e, 4 + p) if q < 6 else result[p] + plane(e3, p)
            block = jnp.concatenate([value[:, 0:128], value[:, 128:256]], 0)
        block = block.T
        for s in range(16):
            at = SLAB[q // 2 * 16 + s] * 16 + 8 * (q % 2)
            packed[at : at + 8, :] = block[8 * s : 8 * s + 8]


def index_of(t, x, y):
    return (t * 4 + x) * 4 + y


def partner(v, first, size):
    return (v + 1) % size if (v - first) % 2 == 0 else (v - 1) % size


def swap_x(dt, first):
    return [
        (index_of(t, x, y), index_of((t + dt) % 16, partner(x, first, 4), y))
        for t in range(16)
        for x in range(4)
        for y in range(4)
    ]


def swap_y(dt, first):
    return [
        (index_of(t, x, y), index_of((t + dt) % 16, x, partner(y, first, 4)))
        for t in range(16)
        for x in range(4)
        for y in range(4)
    ]


def swap_slabs(first):
    return [
        (64 * g + DEVICE[s], 64 * g + DEVICE[partner(s, first, 64)])
        for g in range(4)
        for s in range(64)
    ]


def later():
    return [(d, (d + 16) % 256) for d in range(256)]


def slab_ring(ds, dg=0):
    return [
        (64 * g + DEVICE[s], 64 * ((g + dg) % 4) + DEVICE[(s + ds) % 64])
        for g in range(4)
        for s in range(64)
    ]


def send(value, pairs):
    return lax.ppermute(value, AXES, pairs)


def local(slices_state, forcing, initial, volume, lift):
    tg, tj = lax.axis_index("tg"), lax.axis_index("tj")
    sx, sy = lax.axis_index("sx"), lax.axis_index("sy")
    corner = (sx == 0) & (sy == 0)
    tm = tg * 4 + tj
    flags = jnp.stack(
        [sx > 0, sx < 3, sy > 0, sy < 3, ~(corner & (tj == 0)), ~(corner & (tj == 3))]
        + [tg >= 1, tg >= 2, tg >= 3, tm == 0, tm == 15]
        + [sx % 2 == 0, sy % 2 == 0, tj % 2 == 0]
    ).astype(F32)
    flags = jnp.broadcast_to(flags[:, None], (14, 128))
    lift_flat = jnp.transpose(lift, (1, 0, 2)).reshape(64, 96)
    w = jnp.concatenate([volume, lift_flat], 1)
    face, wide, trace = ((4, 16, 128), F32), ((2, 80, 128), F32), ((2, 16, 128), F32)
    whole, two, rows = ((16, 64, 128), F32), ((4, 64, 128), F32), ((1024, 128), F32)
    (w,) = call(weights_kernel, [((64, 480), BF16)], 0, 1 << 17)(w)

    state = slices_state.reshape(1024, 128)
    source = forcing.reshape(1024, 128)
    start = initial.reshape(1024, 128)
    block = pltpu.VMEM((16, 64, 128), F32)
    faces = call(faces_kernel, [face] * 4, 0, 1 << 19, [block], outs=[(0, 1, EX), (2, 3, EY)])(flags, start, state)
    fine_cost = (2 * 64 * 480 * 2048, 3 << 19)
    v = send(state, later())
    hops = (swap_x(1, 0), swap_x(1, 1), swap_y(1, 0), swap_y(1, 1))
    sides = [(3, 4, EX), (5, 6, EY)]
    for step in range(3):
        xb, xa, yb, ya = [send(f, pairs) for f, pairs in zip(faces, hops)]
        kernel, held, more = (fine_kernel, [], []) if step else (first_fine_kernel, [block], [start])
        v, *faces = call(
            kernel, [whole] + [face] * 4, *fine_cost, held,
            ins=sides, outs=[(1, 2, EX), (3, 4, EY)],
        )(
            flags, v, source, xb, xa, yb, ya, w, *more
        )
        hops = (swap_x(0, 0), swap_x(0, 1), swap_y(0, 0), swap_y(0, 1))
    xb, xa, yb, ya = [send(f, pairs) for f, pairs in zip(faces, hops)]
    resid, packed = call(residual_kernel, [rows, rows], *fine_cost, [block], ins=sides)(
        flags, v, source, xb, xa, yb, ya, w, state
    )

    peers = [[64 * g + d for d in DEVICE] for g in range(4)]

    def traded(value):
        return lax.all_to_all(value, AXES, 0, 0, axis_index_groups=peers, tiled=True)

    received = traded(packed)

    first_swap, second_swap = swap_slabs(0), swap_slabs(1)
    halo_in, halo_out = [(2, 3, EZ)], [(1, 2, EZ)]

    def exchange(pair):
        first, second = pair
        return send(first, first_swap), send(second, second_swap)

    pair_cost = (2 * 64 * 480 * 1536, 1 << 19)
    scratch = [pltpu.VMEM((8, 64, 128), F32), pltpu.VMEM((8, 64, 128), F32)]
    r, *pair = call(
        local_first_kernel, [whole] + [((2, 144, 128), F32)] * 2, 0, 1 << 20, outs=halo_out
    )(flags, received)
    e, *pair = call(
        local_pair_kernel, [((12, 64, 128), F32), trace, trace], *pair_cost, scratch,
        ins=halo_in, outs=halo_out,
    )(
        flags, r, *exchange(pair), w
    )
    (e3,) = call(local_last_kernel, [two], *pair_cost, ins=[(3, 4, EZ)])(flags, e, r, *exchange(pair), w)
    from_3 = send(e3, slab_ring(0, 3))
    from_1 = send(e3, slab_ring(0, 1))
    halos = dict(ins=halo_in, outs=halo_out)
    chain = call(chain_kernel, [two, wide, wide], *pair_cost, scratch, **halos)
    begin = call(begin_kernel, [two, wide, wide], 0, 1 << 18, (), [VM, VM, ANY], outs=halo_out)
    x, *pair = begin(flags, from_3, from_1)
    from_2 = send(from_1, slab_ring(0, 1))
    for which, add in ((FROM_2, from_2), (FROM_1, from_1)):
        x, *pair = chain(flags, x, *exchange(pair), w)
        kernel = functools.partial(chain_add_kernel, which)
        x, *pair = call(kernel, [two, wide, wide], *pair_cost, scratch, **halos)(
            flags, x, *exchange(pair), w, add
        )
    head, x, *pair = call(
        last_first_kernel, [((8, 64, 128), F32), two, wide, wide], *pair_cost, scratch,
        ins=halo_in, outs=[(2, 3, EZ)],
    )(flags, x, *exchange(pair), w, e)
    (packed,) = call(last_second_kernel, [rows], *pair_cost, scratch, ins=halo_in)(
        flags, x, *exchange(pair), w, e, e3, head
    )
    received = traded(packed)
    (corrected,) = call(corrected_kernel, [rows], 0, 3 << 19)(received, state)
    shape = (1, 64, 4, 4, 128)
    return corrected.reshape(shape), resid.reshape(shape)


def solution(mesh):
    fine = Mesh(mesh.devices.reshape(4, 4, 4, 4), AXES)
    time = ("tg", "tj")
    placed = (
        P(time, None, "sx", "sy", None),
        P(time, None, "sx", "sy", None),
        P(None, "sx", "sy", None),
        P(),
        P(),
    )
    return jax.shard_map(
        local,
        mesh=fine,
        in_specs=placed,
        out_specs=(P(time, None, "sx", "sy", None), P(time, None, "sx", "sy", None)),
        check_vma=False,
    )
```

```python
import functools

import jax
import jax.numpy as jnp
from jax import lax
from jax.experimental import pallas as pl
from jax.experimental.pallas import tpu as pltpu
from jax.sharding import Mesh, PartitionSpec as P

F32, BF16 = jnp.float32, jnp.bfloat16
AXES = ("tg", "tj", "sx", "sy")
VM = pl.BlockSpec(memory_space=pltpu.VMEM)
ANY = pl.BlockSpec(memory_space=pl.ANY)
PARAMS = pltpu.CompilerParams(vmem_limit_bytes=40 << 20)
XB, XA, YB, YA, ZB, ZA, FROM_1, FROM_2, FROM_3, FIRST, LAST, EX, EY, EZ = range(14)


def ring_of_slabs():
    path = []
    for x in range(4):
        path += [(0, x, y if x % 2 == 0 else 3 - y) for y in range(4)]
    path += [(1, x, y) for _, x, y in reversed(path)]
    return [(2 * c + k) * 16 + 4 * x + y for c, x, y in path for k in range(2)]


DEVICE = ring_of_slabs()
SLAB = [DEVICE.index(d) for d in range(64)]


def call(kernel, out, flops, nbytes, scratch=(), specs=None, ins=(), outs=()):
    def run(*args):
        extra = [pltpu.VMEM(args[i].shape, F32) for i, j, _ in ins for _ in range(2)]
        extra += [pltpu.VMEM(out[i][0], F32) for i, j, _ in outs for _ in range(2)]

        def body(*refs):
            inner = list(refs[: len(args)])
            outer = list(refs[len(args) : len(args) + len(out)])
            own = refs[len(args) + len(out) : len(args) + len(out) + len(scratch)]
            spare = list(refs[len(args) + len(out) + len(scratch) :])
            flags = inner[0]
            sent = []
            for i, j, row in ins:
                first, second = inner[i], inner[j]
                inner[i], inner[j] = spare.pop(0), spare.pop(0)
                even = flags[row : row + 1, :] > 0.5
                for t in range(first.shape[0]):
                    inner[i][t] = jnp.where(even, second[t], first[t])
                    inner[j][t] = jnp.where(even, first[t], second[t])
            for i, j, row in outs:
                up, down = spare.pop(0), spare.pop(0)
                sent.append((outer[i], outer[j], up, down, row))
                outer[i], outer[j] = up, down
            kernel(*inner, *outer, *own)
            for first, second, up, down, row in sent:
                even = flags[row : row + 1, :] > 0.5
                for t in range(first.shape[0]):
                    first[t] = jnp.where(even, up[t], down[t])
                    second[t] = jnp.where(even, down[t], up[t])

        return pl.pallas_call(
            body,
            out_shape=[jax.ShapeDtypeStruct(s, d) for s, d in out],
            in_specs=specs or [VM] * len(args),
            out_specs=[VM] * len(out),
            scratch_shapes=list(scratch) + extra,
            compiler_params=PARAMS,
            cost_estimate=pl.CostEstimate(flops=flops, bytes_accessed=nbytes, transcendentals=0),
        )(*args)

    return run


def split(value):
    high = value.astype(BF16)
    return high, (value - high.astype(F32)).astype(BF16)


def weights_kernel(w_ref, o_ref):
    high, low = split(w_ref[...])
    o_ref[:, 0:160] = high
    o_ref[:, 160:320] = high
    o_ref[:, 320:480] = low


def product(w, parts):
    high, low = split(jnp.concatenate(parts, 0))
    return jnp.dot(w, jnp.concatenate([high, low, high], 0), preferred_element_type=F32)


def y_trace(ref, b, t):
    return jnp.concatenate([ref[t, 16 * a + 4 * b : 16 * a + 4 * b + 4, :] for a in range(4)], 0)


def z_trace(ref, c, t):
    return ref[t, pl.ds(c, 16, stride=4), :]


def tiles(ref, rows, which):
    return jnp.concatenate([ref[t, rows, :] for t in which], 1)


def flag(flags, which, wide=1):
    return jnp.concatenate([flags[which : which + 1, :]] * wide, 1)


def lanes(shape):
    return lax.broadcasted_iota(jnp.int32, shape, 1)


ALL = slice(None)


def given(ref, t):
    return ref[pl.ds(t, 64, stride=16), :]


def emit_faces(ref, xp, xm, yp, ym):
    for i in range(4):
        xp[i] = ref[12 + i, 48:64, :]
        xm[i] = ref[i, 0:16, :]
        yp[i] = y_trace(ref, 3, 4 * i + 3)
        ym[i] = y_trace(ref, 0, 4 * i)


def gather(flags, which, initial, state, held):
    chosen = flag(flags, which) > 0.5
    for t in range(16):
        held[t] = jnp.where(chosen, given(initial, t), given(state, t))


def faces_kernel(flags, initial, state, xp, xm, yp, ym, held):
    gather(flags, LAST, initial, state, held)
    emit_faces(held, xp, xm, yp, ym)


def fine_step(flags, v, source, xb, xa, yb, ya, w, store):
    weight = w[...]
    lane = lanes((16, 128))
    for i in range(4):
        row = [4 * i + j for j in range(4)]
        own = tiles(v, ALL, row)
        if i == 0:
            below_x = tiles(xb, ALL, range(4)) * flag(flags, XB, 4)
        else:
            below_x = tiles(v, slice(48, 64), [t - 4 for t in row])
        if i == 3:
            above_x = tiles(xa, ALL, range(4)) * flag(flags, XA, 4)
        else:
            above_x = tiles(v, slice(0, 16), [t + 4 for t in row])
        below_y = jnp.concatenate([yb[i] * flag(flags, YB)] + [y_trace(v, 3, t) for t in row[:3]], 1)
        above_y = jnp.concatenate([y_trace(v, 0, t) for t in row[1:]] + [ya[i] * flag(flags, YA)], 1)
        below_z = [jnp.where(lane == 0, 0.0, pltpu.roll(z_trace(v, 3, t), 1, 1)) for t in row]
        above_z = [jnp.where(lane == 127, 0.0, pltpu.roll(z_trace(v, 0, t), 127, 1)) for t in row]
        mixed = product(
            weight,
            [own, below_x, above_x, below_y, above_y]
            + [jnp.concatenate(below_z, 1), jnp.concatenate(above_z, 1)],
        )
        value = (own - 0.1 * own) + mixed
        for j, t in enumerate(row):
            store(t, value[:, 128 * j : 128 * j + 128] + given(source, t))


def first_fine_kernel(flags, v, source, xb, xa, yb, ya, w, initial, out, xp, xm, yp, ym, held):
    gather(flags, FIRST, initial, v, held)
    fine_kernel(flags, held, source, xb, xa, yb, ya, w, out, xp, xm, yp, ym)


def fine_kernel(flags, v, source, xb, xa, yb, ya, w, out, xp, xm, yp, ym):
    def store(t, value):
        out[t] = value

    fine_step(flags, v, source, xb, xa, yb, ya, w, store)
    emit_faces(out, xp, xm, yp, ym)


def residual_kernel(flags, v, source, xb, xa, yb, ya, w, state, out, packed, held):
    def store(t, value):
        value = value - given(state, t)
        out[pl.ds(t, 64, stride=16), :] = value
        held[t] = value

    fine_step(flags, v, source, xb, xa, yb, ya, w, store)
    for m in range(8):
        value = jnp.concatenate([held[2 * m], held[2 * m + 1]], 0).T
        packed[pl.ds(m, 128, stride=8), :] = value


def corrected_kernel(received, state, out):
    for m in range(8):
        block = received[pl.ds(m, 128, stride=8), :].T
        for low in range(2):
            t = 2 * m + low
            out[pl.ds(t, 64, stride=16), :] = block[64 * low : 64 * low + 64] + given(state, t)


def coarse_plane(weight, ref, p, below_z, above_z):
    even, odd = 2 * p, 2 * p + 1
    own = tiles(ref, ALL, (even, odd))
    lane = lanes((16, 128))
    x_high, y_high, x_low, y_low = lane // 32, lane // 8 % 4, lane // 2 % 4, lane % 2

    def moved(value, near, first, far, edge):
        away = jnp.where(edge, 0.0, pltpu.roll(value, far, 1))
        return jnp.where(first, away, pltpu.roll(value, near, 1))

    low_x, top_x = x_low == 0, x_low == 3
    low_y, top_y = y_low == 0, y_low == 1
    below_x = [moved(ref[t, 48:64, :], 2, low_x, 26, x_high == 0) for t in (even, odd)]
    above_x = [moved(ref[t, 0:16, :], 126, top_x, 102, x_high == 3) for t in (even, odd)]
    below_y = [
        moved(y_trace(ref, 3, odd), 1, low_y, 7, y_high == 0),
        y_trace(ref, 3, even),
    ]
    above_y = [
        y_trace(ref, 0, odd),
        moved(y_trace(ref, 0, even), 127, top_y, 121, y_high == 3),
    ]
    sides = [jnp.concatenate(pair, 1) for pair in (below_x, above_x, below_y, above_y)]
    mixed = product(weight, [own] + sides + [below_z, above_z])
    return (own - 0.4 * own) + 4.0 * mixed


def plane(ref, p):
    return tiles(ref, ALL, (2 * p, 2 * p + 1))


def put(ref, p, value, rows=ALL):
    ref[2 * p, rows, :] = value[:, 0:128]
    ref[2 * p + 1, rows, :] = value[:, 128:256]


def z_plane(ref, c, p):
    return jnp.concatenate([z_trace(ref, c, 2 * p), z_trace(ref, c, 2 * p + 1)], 1)


def emit_wide(ref, up, down):
    put(up, 0, plane(ref, 1), slice(0, 64))
    put(up, 0, z_plane(ref, 3, 0), slice(64, 80))
    put(down, 0, plane(ref, 0), slice(0, 64))
    put(down, 0, z_plane(ref, 0, 1), slice(64, 80))


def pair_steps(flags, v, below, above, w, extended, first, add_first, add_second, add_halo):
    weight = w[...]
    has_below, has_above = flag(flags, ZB, 2), flag(flags, ZA, 2)
    both = (0, 1)
    put(extended, 0, tiles(below, slice(0, 64), both) * has_below)
    put(extended, 1, plane(v, 0))
    put(extended, 2, plane(v, 1))
    put(extended, 3, tiles(above, slice(0, 64), both) * has_above)
    for p in range(4):
        if p == 0:
            lower = tiles(below, slice(64, 80), both) * has_below
        else:
            lower = z_plane(extended, 3, p - 1)
        if p == 3:
            upper = tiles(above, slice(64, 80), both) * has_above
        else:
            upper = z_plane(extended, 0, p + 1)
        value = coarse_plane(weight, extended, p, lower, upper)
        if p == 0:
            if add_halo:
                value = value + tiles(below, slice(80, 144), both)
            value = value * has_below
        elif p == 3:
            if add_halo:
                value = value + tiles(above, slice(80, 144), both)
            value = value * has_above
        elif add_first is not None:
            value = value + add_first(p - 1)
        put(first, p, value)
    result = []
    for p in (1, 2):
        value = coarse_plane(weight, first, p, z_plane(first, 3, p - 1), z_plane(first, 0, p + 1))
        result.append(value if add_second is None else value + add_second(p - 1))
    return result


def local_first_kernel(flags, received, r, up, down):
    for q in range(8):
        at = [SLAB[q // 2 * 16 + s] * 16 + 8 * (q % 2) for s in range(16)]
        block = jnp.concatenate([received[a : a + 8, :] for a in at], 0).T
        r[2 * q] = block[0:64]
        r[2 * q + 1] = block[64:128]
    emit_wide(r, up, down)
    put(up, 0, plane(r, 3), slice(80, 144))
    put(down, 0, plane(r, 2), slice(80, 144))


def local_pair_kernel(flags, r, below, above, w, out, up, down, extended, first):
    result = pair_steps(
        flags, r, below, above, w, extended, first,
        lambda p: plane(r, 2 + p), lambda p: plane(r, 4 + p), True,
    )
    for p in range(2):
        put(out, p, plane(r, p))
        put(out, 2 + p, plane(first, 1 + p))
        put(out, 4 + p, result[p])
    put(up, 0, z_plane(out, 3, 5))
    put(down, 0, z_plane(out, 0, 4))


def local_last_kernel(flags, e, r, below, above, w, out):
    weight = w[...]
    for p in range(2):
        lower = plane(below, 0) * flag(flags, ZB, 2) if p == 0 else z_plane(e, 3, 4)
        upper = plane(above, 0) * flag(flags, ZA, 2) if p == 1 else z_plane(e, 0, 5)
        put(out, p, coarse_plane(weight, e, 4 + p, lower, upper) + plane(r, 6 + p))


def chain_kernel(flags, v, below, above, w, out, up, down, extended, first):
    result = pair_steps(flags, v, below, above, w, extended, first, None, None, False)
    for p in range(2):
        put(out, p, result[p])
    emit_wide(out, up, down)


def chain_add_kernel(which, flags, v, below, above, w, add, out, up, down, extended, first):
    chosen = flag(flags, which, 2) > 0.5
    result = pair_steps(
        flags, v, below, above, w, extended, first, None,
        lambda p: jnp.where(chosen, plane(add, p), 0.0), False,
    )
    for p in range(2):
        put(out, p, result[p])
    emit_wide(out, up, down)


def begin_kernel(flags, v, waited, out, up, down):
    for t in range(4):
        out[t] = jnp.where(flag(flags, FROM_3) > 0.5, v[t], 0.0)
    emit_wide(out, up, down)


def last_first_kernel(flags, v, below, above, w, e, out, tail, up, down, extended, first):
    result = pair_steps(flags, v, below, above, w, extended, first, None, None, False)
    for p in range(2):
        put(out, p, plane(first, 1 + p) + plane(e, p))
        put(tail, p, result[p])
        put(out, 2 + p, result[p] + plane(e, 2 + p))
    emit_wide(tail, up, down)


def last_second_kernel(flags, v, below, above, w, e, e3, head, packed, extended, first):
    result = pair_steps(flags, v, below, above, w, extended, first, None, None, False)
    for q in range(8):
        if q < 4:
            block = jnp.concatenate([head[2 * q], head[2 * q + 1]], 0)
        else:
            p = q % 2
            value = plane(first, 1 + p) + plane(e, 4 + p) if q < 6 else result[p] + plane(e3, p)
            block = jnp.concatenate([value[:, 0:128], value[:, 128:256]], 0)
        block = block.T
        for s in range(16):
            at = SLAB[q // 2 * 16 + s] * 16 + 8 * (q % 2)
            packed[at : at + 8, :] = block[8 * s : 8 * s + 8]


def index_of(t, x, y):
    return (t * 4 + x) * 4 + y


def partner(v, first, size):
    return (v + 1) % size if (v - first) % 2 == 0 else (v - 1) % size


def swap_x(dt, first):
    return [
        (index_of(t, x, y), index_of((t + dt) % 16, partner(x, first, 4), y))
        for t in range(16)
        for x in range(4)
        for y in range(4)
    ]


def swap_y(dt, first):
    return [
        (index_of(t, x, y), index_of((t + dt) % 16, x, partner(y, first, 4)))
        for t in range(16)
        for x in range(4)
        for y in range(4)
    ]


def swap_slabs(first):
    return [
        (64 * g + DEVICE[s], 64 * g + DEVICE[partner(s, first, 64)])
        for g in range(4)
        for s in range(64)
    ]


def later():
    return [(d, (d + 16) % 256) for d in range(256)]


def slab_ring(ds, dg=0):
    return [
        (64 * g + DEVICE[s], 64 * ((g + dg) % 4) + DEVICE[(s + ds) % 64])
        for g in range(4)
        for s in range(64)
    ]


def send(value, pairs):
    return lax.ppermute(value, AXES, pairs)


def local(slices_state, forcing, initial, volume, lift):
    tg, tj = lax.axis_index("tg"), lax.axis_index("tj")
    sx, sy = lax.axis_index("sx"), lax.axis_index("sy")
    corner = (sx == 0) & (sy == 0)
    tm = tg * 4 + tj
    flags = jnp.stack(
        [sx > 0, sx < 3, sy > 0, sy < 3, ~(corner & (tj == 0)), ~(corner & (tj == 3))]
        + [tg >= 1, tg >= 2, tg >= 3, tm == 0, tm == 15]
        + [sx % 2 == 0, sy % 2 == 0, tj % 2 == 0]
    ).astype(F32)
    flags = jnp.broadcast_to(flags[:, None], (14, 128))
    lift_flat = jnp.transpose(lift, (1, 0, 2)).reshape(64, 96)
    w = jnp.concatenate([volume, lift_flat], 1)
    face, wide, trace = ((4, 16, 128), F32), ((2, 80, 128), F32), ((2, 16, 128), F32)
    whole, two, rows = ((16, 64, 128), F32), ((4, 64, 128), F32), ((1024, 128), F32)
    (w,) = call(weights_kernel, [((64, 480), BF16)], 0, 1 << 17)(w)

    state = slices_state.reshape(1024, 128)
    source = forcing.reshape(1024, 128)
    start = initial.reshape(1024, 128)
    block = pltpu.VMEM((16, 64, 128), F32)
    faces = call(faces_kernel, [face] * 4, 0, 1 << 19, [block], outs=[(0, 1, EX), (2, 3, EY)])(flags, start, state)
    fine_cost = (2 * 64 * 480 * 2048, 3 << 19)
    v = send(state, later())
    hops = (swap_x(1, 0), swap_x(1, 1), swap_y(1, 0), swap_y(1, 1))
    sides = [(3, 4, EX), (5, 6, EY)]
    for step in range(3):
        xb, yb, xa, ya = [send(faces[i], hops[i]) for i in (0, 2, 1, 3)]
        kernel, held, more = (fine_kernel, [], []) if step else (first_fine_kernel, [block], [start])
        v, *faces = call(
            kernel, [whole] + [face] * 4, *fine_cost, held,
            ins=sides, outs=[(1, 2, EX), (3, 4, EY)],
        )(
            flags, v, source, xb, xa, yb, ya, w, *more
        )
        hops = (swap_x(0, 0), swap_x(0, 1), swap_y(0, 0), swap_y(0, 1))
    xb, yb, xa, ya = [send(faces[i], hops[i]) for i in (0, 2, 1, 3)]
    resid, packed = call(residual_kernel, [rows, rows], *fine_cost, [block], ins=sides)(
        flags, v, source, xb, xa, yb, ya, w, state
    )

    peers = [[64 * g + d for d in DEVICE] for g in range(4)]

    def traded(value):
        return lax.all_to_all(value, AXES, 0, 0, axis_index_groups=peers, tiled=True)

    received = traded(packed)

    first_swap, second_swap = swap_slabs(0), swap_slabs(1)
    halo_in, halo_out = [(2, 3, EZ)], [(1, 2, EZ)]

    def exchange(pair):
        first, second = pair
        return send(first, first_swap), send(second, second_swap)

    pair_cost = (2 * 64 * 480 * 1536, 1 << 19)
    scratch = [pltpu.VMEM((8, 64, 128), F32), pltpu.VMEM((8, 64, 128), F32)]
    r, *pair = call(
        local_first_kernel, [whole] + [((2, 144, 128), F32)] * 2, 0, 1 << 20, outs=halo_out
    )(flags, received)
    e, *pair = call(
        local_pair_kernel, [((12, 64, 128), F32), trace, trace], *pair_cost, scratch,
        ins=halo_in, outs=halo_out,
    )(
        flags, r, *exchange(pair), w
    )
    (e3,) = call(local_last_kernel, [two], *pair_cost, ins=[(3, 4, EZ)])(flags, e, r, *exchange(pair), w)
    from_3 = send(e3, slab_ring(0, 3))
    from_1 = send(e3, slab_ring(0, 1))
    halos = dict(ins=halo_in, outs=halo_out)
    chain = call(chain_kernel, [two, wide, wide], *pair_cost, scratch, **halos)
    begin = call(begin_kernel, [two, wide, wide], 0, 1 << 18, (), [VM, VM, ANY], outs=halo_out)
    x, *pair = begin(flags, from_3, from_1)
    from_2 = send(from_1, slab_ring(0, 1))
    for which, add in ((FROM_2, from_2), (FROM_1, from_1)):
        x, *pair = chain(flags, x, *exchange(pair), w)
        kernel = functools.partial(chain_add_kernel, which)
        x, *pair = call(kernel, [two, wide, wide], *pair_cost, scratch, **halos)(
            flags, x, *exchange(pair), w, add
        )
    head, x, *pair = call(
        last_first_kernel, [((8, 64, 128), F32), two, wide, wide], *pair_cost, scratch,
        ins=halo_in, outs=[(2, 3, EZ)],
    )(flags, x, *exchange(pair), w, e)
    (packed,) = call(last_second_kernel, [rows], *pair_cost, scratch, ins=halo_in)(
        flags, x, *exchange(pair), w, e, e3, head
    )
    received = traded(packed)
    (corrected,) = call(corrected_kernel, [rows], 0, 3 << 19)(received, state)
    shape = (1, 64, 4, 4, 128)
    return corrected.reshape(shape), resid.reshape(shape)


def solution(mesh):
    fine = Mesh(mesh.devices.reshape(4, 4, 4, 4), AXES)
    time = ("tg", "tj")
    placed = (
        P(time, None, "sx", "sy", None),
        P(time, None, "sx", "sy", None),
        P(None, "sx", "sy", None),
        P(),
        P(),
    )
    return jax.shard_map(
        local,
        mesh=fine,
        in_specs=placed,
        out_specs=(P(time, None, "sx", "sy", None), P(time, None, "sx", "sy", None)),
        check_vma=False,
    )
```
